256 devices in a mesh: rec: 32 (over x, y, core), tile: 8 (over z).
Axes of the slice: x: 4, y: 4, z: 8, core: 2. Of those that a mesh axis runs over, the one named last changes fastest.
Arguments:
- deviation: float32 [64, 64, 1024], P(None, 'rec', 'tile'), may hold values from -6 to 6
- footprint: bfloat16 [8192, 8, 2, 8, 8, 128], P('rec', 'tile'), may hold values from -0.046875 to 0.046875
- tile_list: int32 [8192, 8, 2], P('rec', 'tile'), may hold values from -1 to 7, as said below
- offset: int32 [8192], P('rec'), may hold values from 0 to 56
- observed: float32 [8192], P('rec'), may hold values from -10 to 10
- obs_group: int32 [8192], P('rec'), may hold values from 0 to 3
- group_var: float32 [4], replicated, may hold values from 0.5 to 4
- inv_time: float32 [64, 64], replicated, as said below
- inv_lat: float32 [64, 64], replicated, as said below
- inv_lon: float32 [1024, 1024], P('tile'), as said below
Outputs:
- gradient: float32 [64, 64, 1024], P(None, 'rec', 'tile')
- misfit: float32 [8192], P('rec')
The draws below stay inside these ranges and needn't reach their ends.
Inputs may be any that keep to these rules, and one draw needn't show every extreme that they name: `tile_list`: each entry is a latitude tile of 8 rows in the slot's longitude strip, or -1 for an unused slot; the tiles named by one receptor in one strip are distinct. `inv_lon`: symmetric and diagonally dominant with a positive diagonal. `inv_lat`: symmetric and diagonally dominant with a positive diagonal. `inv_time`: symmetric and diagonally dominant with a positive diagonal.
All inputs are finite; a program needn't handle non-finite values.
Results may differ from the reference program's by a relative error of at most 0.0003.
Values sent between devices are 32-bit elements; how exact they have to be, the bound alone decides.
A program may use at most 128 MiB of HBM per device.

```python
import math
import jax
import jax.numpy as jnp
from jax import lax

P_SIZE = 64
W = 8
TY = 8
K = 2
GROUPS = 4
LON_DEV = 128
REC_DEV = 256
NY = 64
NX = 1024
RECEPTORS = 8192
N_REC = 32
N_TILE = 8


def draw_square(key, matrix_order):
    key_one, key_two = jax.random.split(key)
    entries = jax.random.normal(key_one, (matrix_order, matrix_order), jnp.float32)
    entries = entries * (0.8 / matrix_order)
    symmetric = (entries + entries.T) * 0.5
    identity_mat = jnp.eye(matrix_order, dtype=jnp.float32)
    off_diag = symmetric * (1.0 - identity_mat)
    baseline = jax.random.uniform(key_two, (matrix_order,), jnp.float32, 0.5, 1.5)
    diagonal_vals = baseline + jnp.sum(jnp.abs(off_diag), axis=1)
    return off_diag + identity_mat * diagonal_vals[:, None]


def draw_inv_time(key, part):
    return draw_square(jax.random.fold_in(key, 11), P_SIZE)


def draw_inv_lat(key, part):
    return draw_square(jax.random.fold_in(key, 12), NY)


def draw_inv_lon(key, part):
    return draw_square(jax.random.fold_in(key, 13), NX)


def draw_tile_list(key, part):
    tiles_y = NY // TY
    key_one, key_two, key_three = jax.random.split(jax.random.fold_in(key, 14), 3)
    scores = jax.random.randint(key_one, (RECEPTORS, N_TILE, tiles_y), 0, 65536) * tiles_y + jnp.arange(tiles_y, dtype=jnp.int32)
    ranking = jnp.argsort(scores, axis=-1).astype(jnp.int32)[..., :K]
    strip_level = jax.random.randint(key_two, (1, N_TILE, 1), 0, K + 1)
    receptor_extra = jax.random.randint(key_three, (RECEPTORS, N_TILE, 1), 0, K + 1)
    used_count = jnp.minimum(strip_level + receptor_extra, K)
    slot_pos = jnp.arange(K, dtype=jnp.int32)[None, None, :]
    return jnp.where(slot_pos < used_count, ranking, -1).astype(jnp.int32)


def set_ends(drawn, own_key, low, high):
    extent = drawn.shape
    spot = [jax.random.randint(jax.random.fold_in(own_key, axis), (), 0, extent[axis]) for axis in range(len(extent))]
    drawn = drawn.at[tuple(spot)].set(low)
    longest = extent.index(max(extent))
    spot[longest] = (spot[longest] + 1) % extent[longest]
    return drawn.at[tuple(spot)].set(high)


def block_scale(own_key, dims, pieces, smallest, top_value):
    def one(dim, parts):
        heights = jax.random.uniform(jax.random.fold_in(jax.random.fold_in(own_key, 6), dim), (parts,), jnp.float32, smallest / len(pieces), top_value / len(pieces))
        return jnp.repeat(jnp.exp(heights), dims[dim] // parts).reshape((-1,) + (1,) * (len(dims) - dim - 1))

    factor_of = one(*pieces[0])
    for cut in pieces[1:]:
        factor_of = factor_of * one(*cut)
    return factor_of


def noise(own_key, dims, scale, limit, pieces=(), kind=jnp.bfloat16):
    level = block_scale(own_key, dims, pieces, -0.22, 0.18) if pieces else 1.0
    values = jax.random.normal(own_key, dims, jnp.float32) * scale * level
    return jnp.minimum(jnp.maximum(values, -limit), limit).astype(kind)


def setup_inputs(seed: int = 0) -> dict:
    keys = jax.random.split(jax.random.key(seed), 11)
    deviation = noise(keys[0], (P_SIZE, NY, NX), 1.0, 6.0, ((1, 32), (2, 8)), jnp.float32)
    footprint = noise(keys[1], (RECEPTORS, N_TILE, K, W, TY, LON_DEV), (K * W * TY * LON_DEV) ** -0.5, 0.046875, ((0, 32), (1, 8)))
    tile_list = draw_tile_list(jax.random.fold_in(keys[10], 71), 0)
    offset = set_ends(jax.random.randint(keys[3], (RECEPTORS,), 0, P_SIZE - W + 1), jax.random.fold_in(keys[3], 1), 0, P_SIZE - W).astype(jnp.int32)
    observed = noise(keys[4], (RECEPTORS,), 2.0, 10.0, ((0, 32),), jnp.float32)
    obs_group = set_ends(jax.random.randint(keys[5], (RECEPTORS,), 0, GROUPS), jax.random.fold_in(keys[5], 1), 0, GROUPS - 1).astype(jnp.int32)
    group_var = jnp.clip(jnp.exp(jax.random.uniform(keys[6], (GROUPS,), jnp.float32, math.log(0.5), math.log(4.0))), 0.5, 4.0)
    inv_time = draw_inv_time(jax.random.fold_in(keys[10], 71), 0)
    inv_lat = draw_inv_lat(jax.random.fold_in(keys[10], 71), 0)
    inv_lon = draw_inv_lon(jax.random.fold_in(keys[10], 71), 0)
    return dict(deviation=deviation, footprint=footprint, tile_list=tile_list, offset=offset, observed=observed, obs_group=obs_group, group_var=group_var, inv_time=inv_time, inv_lat=inv_lat, inv_lon=inv_lon)


def reference(deviation, footprint, tile_list, offset, observed, obs_group, group_var, inv_time, inv_lat, inv_lon):
    highest = lax.Precision.HIGHEST
    tiles_y = NY // TY
    tile_cells = TY * LON_DEV
    strips = deviation.reshape(P_SIZE, NY, N_TILE, LON_DEV).transpose(2, 0, 1, 3).reshape(N_TILE, P_SIZE * tiles_y, tile_cells)
    active = (tile_list >= 0).astype(jnp.float32)
    starts = offset[:, None] + jnp.arange(W, dtype=jnp.int32)[None, :]
    row_index = (starts[:, None, None, :] * tiles_y + jnp.maximum(tile_list, 0)[:, :, :, None]).astype(jnp.int32)
    groups_foot = footprint.reshape(N_REC, REC_DEV, N_TILE, K, W, tile_cells)
    groups_index = row_index.reshape(N_REC, REC_DEV, N_TILE, K, W)
    groups_active = active.reshape(N_REC, REC_DEV, N_TILE, K)
    strip_ids = jnp.arange(N_TILE, dtype=jnp.int32)[None, :, None, None]

    def forward(element):
        foot_block, row_ids, active_slots = element
        picked = strips[strip_ids, row_ids]
        products = jnp.sum(foot_block.astype(jnp.float32) * picked, axis=(3, 4))
        return jnp.sum(products * active_slots, axis=(1, 2))

    predicted = lax.map(forward, (groups_foot, groups_index, groups_active)).reshape(RECEPTORS)
    variance = group_var[obs_group]
    misfit = (predicted - observed) / variance
    groups_weight = misfit.reshape(N_REC, REC_DEV)[:, :, None, None] * groups_active

    def adjoint(running, element):
        foot_block, row_ids, slot_weight = element
        contrib = foot_block.astype(jnp.float32) * slot_weight[:, :, :, None, None]
        running = running.at[strip_ids, row_ids].add(contrib)
        return running, None

    start_sum = jnp.zeros((N_TILE, P_SIZE * tiles_y, tile_cells), jnp.float32)
    summed, _ = lax.scan(adjoint, start_sum, (groups_foot, groups_index, groups_weight))
    adjoint_field = summed.reshape(N_TILE, P_SIZE, NY, LON_DEV).transpose(1, 2, 0, 3).reshape(P_SIZE, NY, NX)
    lat_done = jnp.einsum("an,pnm->pam", inv_lat, deviation, precision=highest)
    lon_done = jnp.einsum("pam,cm->pac", lat_done, inv_lon, precision=highest)
    time_done = jnp.einsum("qp,pac->qac", inv_time, lon_done, precision=highest)
    return time_done + adjoint_field, misfit
```

```python
import functools

import jax
import jax.numpy as jnp
from jax import lax
from jax.experimental import pallas as pl
from jax.experimental.pallas import tpu as pltpu
from jax.sharding import PartitionSpec as P

MESH = pl.DeviceIdType.MESH
HIGHEST = lax.Precision.HIGHEST
F32 = jnp.float32
VMEM_LIMIT = 48 << 20

SIDE = 4
CORES = 2
PERIODS = 64
HALF = 32
WINDOW = 8
TILES = 8
ROWS = (TILES + 1) * PERIODS
RECEPTORS = 256
STRIPS = 8
CHUNKS = 8
PER_CHUNK = RECEPTORS // CHUNKS
GROUP = 8


def place():
    rec = lax.axis_index("rec")
    return rec // 8, (rec // 2) % SIDE, rec % 2, lax.axis_index("tile")


def rec_of(x, y, c):
    return ((x % SIDE) * SIDE + (y % SIDE)) * CORES + c


def tile_of(x, y):
    return 2 * (x % SIDE) + (y % SIDE) // 2


def pair_of(y, c):
    return pl.multiple_of(4 * ((y % SIDE) % 2) + 2 * c, 2)


def meet(peers):
    barrier = pltpu.get_barrier_semaphore()
    for peer in peers:
        pl.semaphore_signal(barrier, inc=1, device_id=peer, device_id_type=MESH)
    pl.semaphore_wait(barrier, len(peers))


def plane_peers(x, y, c, z):
    peers = [(rec_of(x, y, 1 - c), z)]
    peers += [(rec_of(x + d, y, c), z) for d in (1, 2, 3)]
    peers += [(rec_of(x, y + d, c), z) for d in (1, 2, 3)]
    return peers


def copy_to(src, dst, send, recv, peer):
    return pltpu.make_async_remote_copy(
        src_ref=src, dst_ref=dst, send_sem=send, recv_sem=recv, device_id=peer, device_id_type=MESH
    )


def forward_kernel(
    slots,
    starts,
    group_var,
    dev,
    dev_rows,
    foot,
    observed,
    group,
    inv_time,
    inv_lat,
    inv_lon,
    misfit_out,
    prior_out,
    lat_out,
    strip,
    blocks,
    sums,
    field,
    shares,
    own_share,
    send_sem,
    recv_sem,
    z_send,
    z_recv,
    s_send,
    s_recv,
    f_sem,
    l_sem,
):
    x, y, c, z = place()
    me = rec_of(x, y, c)
    partner = (rec_of(x, y, 1 - c), z)
    loads = []
    for n in range(CHUNKS):
        load = pltpu.make_async_copy(
            foot.at[pl.ds(n * PER_CHUNK, PER_CHUNK), 0], blocks.at[pl.ds(n * PER_CHUNK, PER_CHUNK)], f_sem.at[n]
        )
        load.start()
        loads.append(load)

    def spot(sx, sy, sc, first, count):
        return strip.at[
            pl.ds(pl.multiple_of(PERIODS * (1 + tile_of(sx, sy)) + first, HALF), count), pl.ds(pair_of(sy, sc), 2), :
        ]

    own_local = pltpu.make_async_copy(dev, spot(x, y, c, 0, PERIODS), l_sem.at[0])
    own_local.start()
    own_field = pltpu.make_async_copy(dev_rows, field.at[z], l_sem.at[1])
    own_field.start()
    meet(plane_peers(x, y, c, z) + [(me, (z + d) % STRIPS) for d in range(1, STRIPS)])

    count = [0]
    pending = []

    def send(src, where, peer):
        n = count[0]
        count[0] += 1
        one = copy_to(src, where, send_sem.at[n], recv_sem.at[n], peer)
        one.start()
        pending.append(one)
        return n

    def arrived(n, where):
        copy_to(where, where, send_sem.at[n], recv_sem.at[n], partner).wait_recv()

    first_a, first_b = dev.at[pl.ds(0, HALF)], dev.at[pl.ds(HALF, HALF)]
    in_a = [send(first_a, spot(x, y, c, 0, HALF), (rec_of(x + d, y, c), z)) for d in (1, 2, 3)]
    in_b = [send(first_b, spot(x, y, c, HALF, HALF), (rec_of(x, y + d, c), z)) for d in (1, 2, 3)]
    far_a = [[send(first_a, spot(x, y, c, 0, HALF), (rec_of(x, y + d, c), z)) for d in (1, 2, 3)]]
    far_b = [[send(first_b, spot(x, y, c, HALF, HALF), (rec_of(x + d, y, c), z)) for d in (1, 2, 3)]]
    near = send(dev, spot(x, y, c, 0, PERIODS), partner)
    from_partner = [(near, lambda: spot(x, y, 1 - c, 0, PERIODS))]
    z_copies = []
    for d in range(1, STRIPS):
        one = copy_to(dev_rows, field.at[z], z_send.at[d - 1], z_recv.at[d - 1], (me, (z + d) % STRIPS))
        one.start()
        z_copies.append(one)

    strip[pl.ds(0, PERIODS)] = jnp.zeros((PERIODS, 8, 128), F32)

    wide = (lax.broadcasted_iota(jnp.int32, (2 * PERIODS, PERIODS), 0) // 2
            == lax.broadcasted_iota(jnp.int32, (2 * PERIODS, PERIODS), 1)).astype(F32)
    time_rows = jnp.dot(wide, inv_time[...], precision=HIGHEST, preferred_element_type=F32)
    time_both = lax.dot_general(time_rows, wide, (((1,), (1,)), ((), ())), precision=HIGHEST, preferred_element_type=F32)
    square = (2 * PERIODS, 2 * PERIODS)
    same = lax.broadcasted_iota(jnp.int32, square, 0) % 2 == lax.broadcasted_iota(jnp.int32, square, 1) % 2
    time_both = jnp.where(same, time_both, 0.0)
    for n in range(2):
        pick = (lax.broadcasted_iota(jnp.int32, (64, 128), 0) == 2 * me + n).astype(F32)
        lat_out[n] = jnp.dot(inv_lat[...], pick, precision=HIGHEST, preferred_element_type=F32)

    for d in (1, 2, 3):
        arrived(in_a[d - 1], spot(x - d, y, c, 0, HALF))
        here = spot(x - d, y, c, 0, HALF)
        far_a.append([send(here, here, (rec_of(x, y + e, c), z)) for e in (1, 2, 3)])
        n = send(here, here, partner)
        from_partner.append((n, functools.partial(spot, x - d, y, 1 - c, 0, HALF)))
        arrived(in_b[d - 1], spot(x, y - d, c, HALF, HALF))
        here = spot(x, y - d, c, HALF, HALF)
        far_b.append([send(here, here, (rec_of(x + e, y, c), z)) for e in (1, 2, 3)])
        n = send(here, here, partner)
        from_partner.append((n, functools.partial(spot, x, y - d, 1 - c, HALF, HALF)))
    for d in range(4):
        for e in (1, 2, 3):
            here = spot(x - d, y - e, c, 0, HALF)
            arrived(far_a[d][e - 1], here)
            n = send(here, here, partner)
            from_partner.append((n, functools.partial(spot, x - d, y - e, 1 - c, 0, HALF)))
            here = spot(x - e, y - d, c, HALF, HALF)
            arrived(far_b[d][e - 1], here)
            n = send(here, here, partner)
            from_partner.append((n, functools.partial(spot, x - e, y - d, 1 - c, HALF, HALF)))
    for n, where in from_partner:
        arrived(n, where())
    own_local.wait()
    for load in loads:
        load.wait()

    def group_sums(i, carry):
        totals = []
        for u in range(GROUP):
            r = i * GROUP + u
            start = starts[r]
            parts = []
            for k in range(2):
                base = (slots[k, r] + 1) * PERIODS + start
                parts.append(strip[pl.ds(base, WINDOW)] * blocks[r, k].astype(F32))
            totals.append(jnp.sum(parts[0] + parts[1], axis=0))
        sums[pl.ds(pl.multiple_of(i * GROUP, GROUP), GROUP), :] = jnp.sum(jnp.stack(totals), axis=1)
        return carry

    lax.fori_loop(0, RECEPTORS // GROUP, group_sums, 0)
    share = lax.dot_general(
        jnp.ones((8, 128), F32), sums[...], (((1,), (1,)), ((), ())), precision=HIGHEST, preferred_element_type=F32
    )
    own_share[...] = share
    s_copies = []
    for d in range(1, STRIPS):
        one = copy_to(
            own_share.at[pl.ds(0, 1), :], shares.at[pl.ds(z, 1), :], s_send.at[d - 1], s_recv.at[d - 1],
            (me, (z + d) % STRIPS),
        )
        one.start()
        s_copies.append(one)
    mine = pltpu.make_async_copy(own_share.at[pl.ds(0, 1), :], shares.at[pl.ds(z, 1), :], l_sem.at[2])
    mine.start()

    own_field.wait()
    for one in z_copies:
        one.wait()
    lon_done = jnp.zeros((2 * PERIODS, 128), F32)
    for s in range(STRIPS):
        lon_done += lax.dot_general(
            field[s], inv_lon[:, s * 128 : (s + 1) * 128], (((1,), (1,)), ((), ())),
            precision=HIGHEST, preferred_element_type=F32,
        )
    prior_out[...] = jnp.dot(time_both, lon_done, precision=HIGHEST, preferred_element_type=F32)

    mine.wait()
    for one in s_copies:
        one.wait()
    predicted = jnp.sum(shares[...], axis=0, keepdims=True)
    variance = jnp.zeros((1, RECEPTORS), F32)
    for g in range(4):
        variance += jnp.where(group[...] == g, group_var[g], 0.0)
    misfit_out[...] = (predicted - observed[...]) / variance
    for one in pending:
        one.wait_send()


def adjoint_kernel(slots, starts, misfit, foot, prior, lat, misfit_row, total, misfit_out, blocks, second, f_sem):
    loads = []
    for n in range(CHUNKS):
        load = pltpu.make_async_copy(
            foot.at[pl.ds(n * PER_CHUNK, PER_CHUNK), 0], blocks.at[pl.ds(n * PER_CHUNK, PER_CHUNK)], f_sem.at[n]
        )
        load.start()
        loads.append(load)
    misfit_out[...] = misfit_row[...]
    second[...] = jnp.zeros((ROWS, 8, 128), F32)
    total[pl.ds(0, PERIODS)] = jnp.zeros((PERIODS, 8, 128), F32)

    def one_period(p, carry):
        first = jnp.broadcast_to(prior[pl.ds(2 * p, 1), :], (8, 128))
        other = jnp.broadcast_to(prior[pl.ds(2 * p + 1, 1), :], (8, 128))
        for t in range(TILES):
            rows = slice(8 * t, 8 * t + 8)
            total[PERIODS * (1 + t) + p] = lat[0, rows, :] * first + lat[1, rows, :] * other
        return carry

    lax.fori_loop(0, PERIODS, one_period, 0)

    def pair(i, carry):
        held = []
        for u, into in ((0, total), (1, second)):
            r = 2 * i + u
            start = starts[r]
            weight = misfit[r]
            for k in range(2):
                rows = pl.ds((slots[k, r] + 1) * PERIODS + start, WINDOW)
                held.append((into, rows, into[rows] + blocks[r, k].astype(F32) * weight))
        for into, rows, value in held:
            into[rows] = value
        return carry

    for n in range(CHUNKS):
        loads[n].wait()
        lax.fori_loop(n * PER_CHUNK // 2, (n + 1) * PER_CHUNK // 2, pair, 0)

    def join(i, carry):
        rows = pl.ds(pl.multiple_of(PERIODS + i * 16, 16), 16)
        total[rows] = total[rows] + second[rows]
        return carry

    lax.fori_loop(0, TILES * PERIODS // 16, join, 0)


def scatter_kernel(
    part, out, got, both, a_got, a_sum, a_last, b_got, b_sum, b_last, done, e_send, e_recv, send_sem, recv_sem, l_sem
):
    x, y, c, z = place()
    partner = (rec_of(x, y, 1 - c), z)
    meet(plane_peers(x, y, c, z))
    swaps = []
    for half in range(2):
        for h in range(2):
            n = 2 * half + h
            theirs = pl.ds(pl.multiple_of(4 * h + 2 * (1 - c), 2), 2)
            periods = pl.ds(half * HALF, HALF)
            one = copy_to(
                part.at[pl.ds(1, TILES), periods, theirs, :], got.at[:, periods, theirs, :],
                e_send.at[n], e_recv.at[n], partner,
            )
            one.start()
            swaps.append(one)
    my_tile = tile_of(x, y)
    my_th = y // 2
    my_pair = pl.ds(pair_of(y, c), 2)
    pending = []

    def send(n, src, dst, peer):
        one = copy_to(src, dst, send_sem.at[n], recv_sem.at[n], peer)
        one.start()
        pending.append(one)
        return one

    def add_half(half):
        def step(t, carry):
            periods = pl.ds(half * HALF, HALF)
            both[t, periods] = part[1 + t, periods] + got[t, periods]
            return carry

        lax.fori_loop(0, TILES, step, 0)

    swaps[0].wait_recv()
    swaps[1].wait_recv()
    add_half(0)
    a_copies = []
    for d in (1, 2, 3):
        for h in range(2):
            rows = pl.ds(pl.multiple_of(4 * h + 2 * c, 2), 2)
            a_copies.append(send(
                2 * (d - 1) + h,
                both.at[pl.ds(2 * ((x + d) % SIDE), 2), pl.ds(0, HALF), rows, :],
                a_got.at[d - 1, :, :, rows, :],
                (rec_of(x + d, y, c), z),
            ))
    swaps[2].wait_recv()
    swaps[3].wait_recv()
    add_half(1)
    b_copies = []
    for d in (1, 2, 3):
        rows = pl.ds(pair_of(y + d, c), 2)
        for s in range(SIDE):
            b_copies.append(send(
                6 + 4 * (d - 1) + s,
                both.at[2 * s + ((y + d) % SIDE) // 2, pl.ds(HALF, HALF), rows, :],
                b_got.at[d - 1, s, :, rows, :],
                (rec_of(x, y + d, c), z),
            ))
    for one in a_copies:
        one.wait_recv()
    for th in range(2):
        a_sum[th] = both[2 * x + th, pl.ds(0, HALF)] + a_got[0, th] + a_got[1, th] + a_got[2, th]
    a_final = []
    for d in (1, 2, 3):
        rows = pl.ds(pair_of(y + d, c), 2)
        a_final.append(send(
            18 + d - 1, a_sum.at[((y + d) % SIDE) // 2, :, rows, :], a_last.at[d - 1, :, rows, :],
            (rec_of(x, y + d, c), z),
        ))
    for one in b_copies:
        one.wait_recv()
    for s in range(SIDE):
        b_sum[s] = both[2 * s + my_th, pl.ds(HALF, HALF)] + b_got[0, s] + b_got[1, s] + b_got[2, s]
    b_final = []
    for d in (1, 2, 3):
        b_final.append(send(
            21 + d - 1, b_sum.at[(x + d) % SIDE, :, my_pair, :], b_last.at[d - 1, :, my_pair, :],
            (rec_of(x + d, y, c), z),
        ))
    for one in a_final:
        one.wait_recv()
    done[pl.ds(0, HALF)] = a_sum[my_th] + a_last[0] + a_last[1] + a_last[2]
    for one in b_final:
        one.wait_recv()
    done[pl.ds(HALF, HALF)] = b_sum[x] + b_last[0] + b_last[1] + b_last[2]
    final = pltpu.make_async_copy(done.at[:, my_pair, :], out, l_sem)
    final.start()
    for one in swaps + pending:
        one.wait_send()
    final.wait()


def shards(
    deviation, footprint, tile_list, offset, observed, obs_group, group_var, inv_time, inv_lat, inv_lon
):
    vmem = pl.BlockSpec(memory_space=pltpu.VMEM)
    smem = pl.BlockSpec(memory_space=pltpu.SMEM)
    hbm = pl.BlockSpec(memory_space=pl.ANY)
    slots = jnp.transpose(tile_list, (1, 2, 0)).reshape(2, RECEPTORS)
    copies = 61
    misfit_row, prior, lat = pl.pallas_call(
        forward_kernel,
        name="forward",
        out_shape=(
            jax.ShapeDtypeStruct((1, RECEPTORS), F32),
            jax.ShapeDtypeStruct((2 * PERIODS, 128), F32),
            jax.ShapeDtypeStruct((2, 64, 128), F32),
        ),
        in_specs=[smem, smem, smem, vmem, vmem, hbm, vmem, vmem, vmem, vmem, vmem],
        out_specs=(vmem, vmem, vmem),
        scratch_shapes=[
            pltpu.VMEM((ROWS, 8, 128), F32),
            pltpu.VMEM((RECEPTORS, 2, WINDOW, 8, 128), jnp.bfloat16),
            pltpu.VMEM((RECEPTORS, 128), F32),
            pltpu.VMEM((STRIPS, 2 * PERIODS, 128), F32),
            pltpu.VMEM((STRIPS, RECEPTORS), F32),
            pltpu.VMEM((8, RECEPTORS), F32),
            pltpu.SemaphoreType.DMA((copies,)),
            pltpu.SemaphoreType.DMA((copies,)),
            pltpu.SemaphoreType.DMA((7,)),
            pltpu.SemaphoreType.DMA((7,)),
            pltpu.SemaphoreType.DMA((7,)),
            pltpu.SemaphoreType.DMA((7,)),
            pltpu.SemaphoreType.DMA((CHUNKS,)),
            pltpu.SemaphoreType.DMA((3,)),
        ],
        compiler_params=pltpu.CompilerParams(collective_id=0, has_side_effects=True, vmem_limit_bytes=VMEM_LIMIT),
    )(
        slots,
        offset,
        group_var,
        deviation,
        deviation.reshape(2 * PERIODS, 128),
        footprint,
        observed.reshape(1, RECEPTORS),
        obs_group.reshape(1, RECEPTORS),
        inv_time,
        inv_lat,
        inv_lon,
    )
    total, misfit = pl.pallas_call(
        adjoint_kernel,
        name="adjoint",
        out_shape=(jax.ShapeDtypeStruct((ROWS, 8, 128), F32), jax.ShapeDtypeStruct((1, RECEPTORS), F32)),
        in_specs=[smem, smem, smem, hbm, vmem, vmem, vmem],
        out_specs=(vmem, vmem),
        scratch_shapes=[
            pltpu.VMEM((RECEPTORS, 2, WINDOW, 8, 128), jnp.bfloat16),
            pltpu.VMEM((ROWS, 8, 128), F32),
            pltpu.SemaphoreType.DMA((CHUNKS,)),
        ],
        compiler_params=pltpu.CompilerParams(vmem_limit_bytes=VMEM_LIMIT),
    )(slots, offset, misfit_row.reshape(RECEPTORS), footprint, prior, lat, misfit_row)
    gradient = pl.pallas_call(
        scatter_kernel,
        name="scatter",
        out_shape=jax.ShapeDtypeStruct((PERIODS, 2, 128), F32),
        in_specs=[vmem],
        out_specs=hbm,
        scratch_shapes=[
            pltpu.VMEM((TILES, PERIODS, 8, 128), F32),
            pltpu.VMEM((TILES, PERIODS, 8, 128), F32),
            pltpu.VMEM((3, 2, HALF, 8, 128), F32),
            pltpu.VMEM((2, HALF, 8, 128), F32),
            pltpu.VMEM((3, HALF, 8, 128), F32),
            pltpu.VMEM((3, SIDE, HALF, 8, 128), F32),
            pltpu.VMEM((SIDE, HALF, 8, 128), F32),
            pltpu.VMEM((3, HALF, 8, 128), F32),
            pltpu.VMEM((PERIODS, 8, 128), F32),
            pltpu.SemaphoreType.DMA((4,)),
            pltpu.SemaphoreType.DMA((4,)),
            pltpu.SemaphoreType.DMA((24,)),
            pltpu.SemaphoreType.DMA((24,)),
            pltpu.SemaphoreType.DMA,
        ],
        compiler_params=pltpu.CompilerParams(collective_id=1, has_side_effects=True, vmem_limit_bytes=VMEM_LIMIT),
    )(total.reshape(TILES + 1, PERIODS, 8, 128))
    return gradient, misfit.reshape(RECEPTORS)


def solution(mesh):
    return jax.shard_map(
        shards,
        mesh=mesh,
        in_specs=(
            P(None, "rec", "tile"),
            P("rec", "tile", None, None, None, None),
            P("rec", "tile", None),
            P("rec"),
            P("rec"),
            P("rec"),
            P(),
            P(),
            P(),
            P("tile", None),
        ),
        out_specs=(P(None, "rec", "tile"), P("rec")),
        check_vma=False,
    )
```

```python
import functools

import jax
import jax.numpy as jnp
from jax import lax
from jax.experimental import pallas as pl
from jax.experimental.pallas import tpu as pltpu
from jax.sharding import PartitionSpec as P

MESH = pl.DeviceIdType.MESH
HIGHEST = lax.Precision.HIGHEST
F32 = jnp.float32
VMEM_LIMIT = 28 << 20

SIDE = 4
CORES = 2
PERIODS = 64
HALF = 32
WINDOW = 8
TILES = 8
ROWS = (TILES + 1) * PERIODS
SUM_ROWS = (TILES + 2) * PERIODS
RECEPTORS = 256
STRIPS = 8
CHUNKS = 8
PER_CHUNK = RECEPTORS // CHUNKS
GROUP = 8


def place():
    rec = lax.axis_index("rec")
    return rec // 8, (rec // 2) % SIDE, rec % 2, lax.axis_index("tile")


def rec_of(x, y, c):
    return ((x % SIDE) * SIDE + (y % SIDE)) * CORES + c


def tile_of(x, y):
    return 2 * (x % SIDE) + (y % SIDE) // 2


def pair_of(y, c):
    return pl.multiple_of(4 * ((y % SIDE) % 2) + 2 * c, 2)


def in_hbm(value):
    return pltpu.with_memory_space_constraint(value, pltpu.HBM)


def meet(peers):
    barrier = pltpu.get_barrier_semaphore()
    for peer in peers:
        pl.semaphore_signal(barrier, inc=1, device_id=peer, device_id_type=MESH)
    pl.semaphore_wait(barrier, len(peers))


def plane_peers(x, y, c, z):
    peers = [(rec_of(x, y, 1 - c), z)]
    peers += [(rec_of(x + d, y, c), z) for d in (1, 2, 3)]
    peers += [(rec_of(x, y + d, c), z) for d in (1, 2, 3)]
    return peers


def copy_to(src, dst, send, recv, peer):
    return pltpu.make_async_remote_copy(
        src_ref=src, dst_ref=dst, send_sem=send, recv_sem=recv, device_id=peer, device_id_type=MESH
    )


def forward_kernel(
    slots_hbm,
    starts_hbm,
    group_var_hbm,
    dev,
    dev_rows,
    foot,
    observed_hbm,
    group_hbm,
    inv_time_hbm,
    inv_lat_hbm,
    inv_lon_hbm,
    misfit_out,
    prior_out,
    lat_out,
    blocks,
    slots,
    starts,
    group_var,
    observed,
    group,
    inv_time,
    inv_lat,
    inv_lon,
    i_sem,
    strip,
    sums,
    field,
    shares,
    own_share,
    send_sem,
    recv_sem,
    z_send,
    z_recv,
    s_send,
    s_recv,
    f_sem,
    l_sem,
):
    x, y, c, z = place()
    me = rec_of(x, y, c)
    partner = (rec_of(x, y, 1 - c), z)
    small = []
    for n, (src, dst) in enumerate((
        (inv_time_hbm, inv_time), (inv_lat_hbm, inv_lat), (slots_hbm, slots), (starts_hbm, starts),
        (group_var_hbm, group_var), (observed_hbm, observed), (group_hbm, group), (inv_lon_hbm, inv_lon),
    )):
        load = pltpu.make_async_copy(src, dst, i_sem.at[n])
        load.start()
        small.append(load)

    def spot(sx, sy, sc, first, count):
        return strip.at[
            pl.ds(pl.multiple_of(PERIODS * (1 + tile_of(sx, sy)) + first, HALF), count), pl.ds(pair_of(sy, sc), 2), :
        ]

    own_local = pltpu.make_async_copy(dev, spot(x, y, c, 0, PERIODS), l_sem.at[0])
    own_local.start()
    own_field = pltpu.make_async_copy(dev_rows, field.at[z], l_sem.at[1])
    own_field.start()
    meet(plane_peers(x, y, c, z) + [(me, (z + d) % STRIPS) for d in range(1, STRIPS)])

    count = [0]
    pending = []

    def send(src, where, peer):
        n = count[0]
        count[0] += 1
        one = copy_to(src, where, send_sem.at[n], recv_sem.at[n], peer)
        one.start()
        pending.append(one)
        return n

    def arrived(n, where):
        copy_to(where, where, send_sem.at[n], recv_sem.at[n], partner).wait_recv()

    first_a, first_b = dev.at[pl.ds(0, HALF)], dev.at[pl.ds(HALF, HALF)]
    in_a = [send(first_a, spot(x, y, c, 0, HALF), (rec_of(x + d, y, c), z)) for d in (1, 2, 3)]
    in_b = [send(first_b, spot(x, y, c, HALF, HALF), (rec_of(x, y + d, c), z)) for d in (1, 2, 3)]
    far_a = [[send(first_a, spot(x, y, c, 0, HALF), (rec_of(x, y + d, c), z)) for d in (1, 2, 3)]]
    far_b = [[send(first_b, spot(x, y, c, HALF, HALF), (rec_of(x + d, y, c), z)) for d in (1, 2, 3)]]
    near = send(dev, spot(x, y, c, 0, PERIODS), partner)
    from_partner = [(near, lambda: spot(x, y, 1 - c, 0, PERIODS))]
    z_copies = []
    for d in range(1, STRIPS):
        one = copy_to(dev_rows, field.at[z], z_send.at[d - 1], z_recv.at[d - 1], (me, (z + d) % STRIPS))
        one.start()
        z_copies.append(one)

    loads = []
    for n in range(CHUNKS):
        load = pltpu.make_async_copy(
            foot.at[pl.ds(n * PER_CHUNK, PER_CHUNK), 0], blocks.at[pl.ds(n * PER_CHUNK, PER_CHUNK)], f_sem.at[n]
        )
        load.start()
        loads.append(load)
    strip[pl.ds(0, PERIODS)] = jnp.zeros((PERIODS, 8, 128), F32)
    for load in small:
        load.wait()

    wide = (lax.broadcasted_iota(jnp.int32, (2 * PERIODS, PERIODS), 0) // 2
            == lax.broadcasted_iota(jnp.int32, (2 * PERIODS, PERIODS), 1)).astype(F32)
    time_rows = jnp.dot(wide, inv_time[...], precision=HIGHEST, preferred_element_type=F32)
    time_both = lax.dot_general(time_rows, wide, (((1,), (1,)), ((), ())), precision=HIGHEST, preferred_element_type=F32)
    square = (2 * PERIODS, 2 * PERIODS)
    same = lax.broadcasted_iota(jnp.int32, square, 0) % 2 == lax.broadcasted_iota(jnp.int32, square, 1) % 2
    time_both = jnp.where(same, time_both, 0.0)
    for n in range(2):
        pick = (lax.broadcasted_iota(jnp.int32, (64, 128), 0) == 2 * me + n).astype(F32)
        lat_out[n] = jnp.dot(inv_lat[...], pick, precision=HIGHEST, preferred_element_type=F32)

    for d in (1, 2, 3):
        arrived(in_a[d - 1], spot(x - d, y, c, 0, HALF))
        here = spot(x - d, y, c, 0, HALF)
        far_a.append([send(here, here, (rec_of(x, y + e, c), z)) for e in (1, 2, 3)])
        n = send(here, here, partner)
        from_partner.append((n, functools.partial(spot, x - d, y, 1 - c, 0, HALF)))
        arrived(in_b[d - 1], spot(x, y - d, c, HALF, HALF))
        here = spot(x, y - d, c, HALF, HALF)
        far_b.append([send(here, here, (rec_of(x + e, y, c), z)) for e in (1, 2, 3)])
        n = send(here, here, partner)
        from_partner.append((n, functools.partial(spot, x, y - d, 1 - c, HALF, HALF)))
    for d in range(4):
        for e in (1, 2, 3):
            here = spot(x - d, y - e, c, 0, HALF)
            arrived(far_a[d][e - 1], here)
            n = send(here, here, partner)
            from_partner.append((n, functools.partial(spot, x - d, y - e, 1 - c, 0, HALF)))
            here = spot(x - e, y - d, c, HALF, HALF)
            arrived(far_b[d][e - 1], here)
            n = send(here, here, partner)
            from_partner.append((n, functools.partial(spot, x - e, y - d, 1 - c, HALF, HALF)))
    for n, where in from_partner:
        arrived(n, where())
    own_local.wait()
    for load in loads:
        load.wait()

    def group_sums(i, carry):
        totals = []
        for u in range(GROUP):
            r = i * GROUP + u
            start = starts[r]
            parts = []
            for k in range(2):
                base = (slots[k, r] + 1) * PERIODS + start
                parts.append(strip[pl.ds(base, WINDOW)] * blocks[r, k].astype(F32))
            totals.append(jnp.sum(parts[0] + parts[1], axis=0))
        sums[pl.ds(pl.multiple_of(i * GROUP, GROUP), GROUP), :] = jnp.sum(jnp.stack(totals), axis=1)
        return carry

    lax.fori_loop(0, RECEPTORS // GROUP, group_sums, 0)
    share = lax.dot_general(
        jnp.ones((8, 128), F32), sums[...], (((1,), (1,)), ((), ())), precision=HIGHEST, preferred_element_type=F32
    )
    own_share[...] = share
    s_copies = []
    for d in range(1, STRIPS):
        one = copy_to(
            own_share.at[pl.ds(0, 1), :], shares.at[pl.ds(z, 1), :], s_send.at[d - 1], s_recv.at[d - 1],
            (me, (z + d) % STRIPS),
        )
        one.start()
        s_copies.append(one)
    mine = pltpu.make_async_copy(own_share.at[pl.ds(0, 1), :], shares.at[pl.ds(z, 1), :], l_sem.at[2])
    mine.start()

    own_field.wait()
    for one in z_copies:
        one.wait()
    lon_done = jnp.zeros((2 * PERIODS, 128), F32)
    for s in range(STRIPS):
        lon_done += lax.dot_general(
            field[s], inv_lon[:, s * 128 : (s + 1) * 128], (((1,), (1,)), ((), ())),
            precision=HIGHEST, preferred_element_type=F32,
        )
    prior_out[...] = jnp.dot(time_both, lon_done, precision=HIGHEST, preferred_element_type=F32)

    mine.wait()
    for one in s_copies:
        one.wait()
    predicted = jnp.sum(shares[...], axis=0, keepdims=True)
    variance = jnp.zeros((1, RECEPTORS), F32)
    for g in range(4):
        variance += jnp.where(group[...] == g, group_var[g], 0.0)
    misfit_out[...] = (predicted - observed[...]) / variance
    for one in pending:
        one.wait_send()


def adjoint_kernel(
    slots_hbm, starts_hbm, misfit_hbm, blocks, misfit_row, total, second, misfit_out, slots, starts, misfit, i_sem
):
    small = []
    for n, (src, dst) in enumerate(((slots_hbm, slots), (starts_hbm, starts), (misfit_hbm, misfit))):
        load = pltpu.make_async_copy(src, dst, i_sem.at[n])
        load.start()
        small.append(load)
    misfit_out[...] = misfit_row[...]

    def clear(i, carry):
        rows = pl.ds(pl.multiple_of(i * 16, 16), 16)
        total[rows] = jnp.zeros((16, 8, 128), F32)
        second[rows] = jnp.zeros((16, 8, 128), F32)
        return carry

    lax.fori_loop(0, SUM_ROWS // 16, clear, 0)
    for load in small:
        load.wait()

    def pair(i, carry):
        held = []
        for u, into in ((0, total), (1, second)):
            r = 2 * i + u
            start = starts[r]
            weight = misfit[r]
            for k in range(2):
                rows = pl.ds((slots[k, r] + 2) * PERIODS + start, WINDOW)
                held.append((into, rows, into[rows] + blocks[r, k].astype(F32) * weight))
        for into, rows, value in held:
            into[rows] = value
        return carry

    lax.fori_loop(0, RECEPTORS // 2, pair, 0)


ORDER = (2, 1, 3, 0)


def scatter_kernel(
    total, second, prior, lat, out, part, a_swap, a_both, a_got, a_sum, a_last, b_swap, b_both, b_got, b_sum, b_last,
    done, send_sem, recv_sem, l_sem,
):
    x, y, c, z = place()
    partner = (rec_of(x, y, 1 - c), z)
    barrier = pltpu.get_barrier_semaphore()
    peers = plane_peers(x, y, c, z)
    for peer in peers:
        pl.semaphore_signal(barrier, inc=1, device_id=peer, device_id_type=MESH)

    def one_period(p, carry):
        first = jnp.broadcast_to(prior[pl.ds(2 * p, 1), :], (8, 128))
        other = jnp.broadcast_to(prior[pl.ds(2 * p + 1, 1), :], (8, 128))
        for t in range(TILES):
            rows = slice(8 * t, 8 * t + 8)
            part[t // 2, t % 2, p] = (
                total[1 + t // 2, t % 2, p] + second[1 + t // 2, t % 2, p]
                + (lat[0, rows, :] * first + lat[1, rows, :] * other)
            )
        return carry

    lax.fori_loop(0, PERIODS, one_period, 0)
    pl.semaphore_wait(barrier, len(peers))

    first_half, second_half = pl.ds(0, HALF), pl.ds(HALF, HALF)
    count = [0]
    pending = []

    def send(src, dst, peer):
        n = count[0]
        count[0] += 1
        one = copy_to(src, dst, send_sem.at[n], recv_sem.at[n], peer)
        one.start()
        pending.append(one)
        return one

    def pair_rows(sy, sc):
        return pl.ds(pair_of(sy, sc), 2)

    def half_of(sy):
        return (sy % SIDE) // 2

    mine = pair_rows(y, c)
    swaps = {}
    for e in ORDER:
        theirs = pair_rows(y + e, 1 - c)
        a = [send(part.at[:, half_of(y + e), first_half, theirs, :], a_swap.at[e, :, :, theirs, :], partner)]
        b = []
        for h in range(2):
            rows = pl.ds(pl.multiple_of(4 * h + 2 * (1 - c), 2), 2)
            b.append(send(part.at[(x + e) % SIDE, :, second_half, rows, :], b_swap.at[e, :, :, rows, :], partner))
        swaps[e] = (a, b)
    a_copies, b_copies = {}, {}
    for e in ORDER:
        for one in swaps[e][0]:
            one.wait_recv()
        for s in range(SIDE):
            a_both[e, s] = part[s, half_of(y + e), first_half] + a_swap[e, s]
        rows = pair_rows(y + e, c)
        a_copies[e] = [
            send(a_both.at[e, (x + d) % SIDE, :, rows, :], a_got.at[e, d - 1, :, rows, :], (rec_of(x + d, y, c), z))
            for d in (2, 1, 3)
        ]
        for one in swaps[e][1]:
            one.wait_recv()
        for th in range(2):
            b_both[e, th] = part[(x + e) % SIDE, th, second_half] + b_swap[e, th]
        b_copies[e] = [
            send(
                b_both.at[e, half_of(y + d), :, pair_rows(y + d, c), :],
                b_got.at[e, d - 1, :, pair_rows(y + d, c), :],
                (rec_of(x, y + d, c), z),
            )
            for d in (2, 1, 3)
        ]
    a_final, b_final = [], []
    for e in ORDER:
        for one in a_copies[e]:
            one.wait_recv()
        a_total = a_both[e, x] + a_got[e, 0] + a_got[e, 1] + a_got[e, 2]
        if e:
            rows = pair_rows(y + e, c)
            a_sum[e - 1] = a_total
            a_final.append(
                send(a_sum.at[e - 1, :, rows, :], a_last.at[e - 1, :, rows, :], (rec_of(x, y + e, c), z))
            )
        else:
            done[first_half] = a_total
        for one in b_copies[e]:
            one.wait_recv()
        b_total = b_both[e, half_of(y)] + b_got[e, 0] + b_got[e, 1] + b_got[e, 2]
        if e:
            b_sum[e - 1] = b_total
            b_final.append(
                send(b_sum.at[e - 1, :, mine, :], b_last.at[e - 1, :, mine, :], (rec_of(x + e, y, c), z))
            )
        else:
            done[second_half] = b_total
    for one in a_final:
        one.wait_recv()
    done[first_half] = done[first_half] + a_last[0] + a_last[1] + a_last[2]
    for one in b_final:
        one.wait_recv()
    done[second_half] = done[second_half] + b_last[0] + b_last[1] + b_last[2]
    final = pltpu.make_async_copy(done.at[:, mine, :], out, l_sem)
    final.start()
    for one in pending:
        one.wait_send()
    final.wait()


def shards(
    deviation, footprint, tile_list, offset, observed, obs_group, group_var, inv_time, inv_lat, inv_lon
):
    vmem = pl.BlockSpec(memory_space=pltpu.VMEM)
    hbm = pl.BlockSpec(memory_space=pltpu.HBM)
    slots = jnp.transpose(tile_list, (1, 2, 0)).reshape(2, RECEPTORS)
    copies = 61
    misfit_row, prior, lat, blocks = pl.pallas_call(
        forward_kernel,
        name="forward",
        out_shape=(
            jax.ShapeDtypeStruct((1, RECEPTORS), F32),
            jax.ShapeDtypeStruct((2 * PERIODS, 128), F32),
            jax.ShapeDtypeStruct((2, 64, 128), F32),
            jax.ShapeDtypeStruct((RECEPTORS, 2, WINDOW, 8, 128), jnp.bfloat16),
        ),
        in_specs=[hbm] * 11,
        out_specs=(vmem, vmem, vmem, vmem),
        scratch_shapes=[
            pltpu.SMEM((2, RECEPTORS), jnp.int32),
            pltpu.SMEM((RECEPTORS,), jnp.int32),
            pltpu.SMEM((4,), F32),
            pltpu.VMEM((1, RECEPTORS), F32),
            pltpu.VMEM((1, RECEPTORS), jnp.int32),
            pltpu.VMEM((PERIODS, PERIODS), F32),
            pltpu.VMEM((64, 64), F32),
            pltpu.VMEM((128, 1024), F32),
            pltpu.SemaphoreType.DMA((8,)),
            pltpu.VMEM((ROWS, 8, 128), F32),
            pltpu.VMEM((RECEPTORS, 128), F32),
            pltpu.VMEM((STRIPS, 2 * PERIODS, 128), F32),
            pltpu.VMEM((STRIPS, RECEPTORS), F32),
            pltpu.VMEM((8, RECEPTORS), F32),
            pltpu.SemaphoreType.DMA((copies,)),
            pltpu.SemaphoreType.DMA((copies,)),
            pltpu.SemaphoreType.DMA((7,)),
            pltpu.SemaphoreType.DMA((7,)),
            pltpu.SemaphoreType.DMA((7,)),
            pltpu.SemaphoreType.DMA((7,)),
            pltpu.SemaphoreType.DMA((CHUNKS,)),
            pltpu.SemaphoreType.DMA((3,)),
        ],
        compiler_params=pltpu.CompilerParams(collective_id=0, has_side_effects=True, vmem_limit_bytes=VMEM_LIMIT),
    )(
        *map(in_hbm, (
            slots,
            offset,
            group_var,
            deviation,
            deviation.reshape(2 * PERIODS, 128),
            footprint,
            observed.reshape(1, RECEPTORS),
            obs_group.reshape(1, RECEPTORS),
            inv_time,
            inv_lat,
            inv_lon,
        ))
    )
    total, second, misfit = pl.pallas_call(
        adjoint_kernel,
        name="adjoint",
        out_shape=(
            jax.ShapeDtypeStruct((SUM_ROWS, 8, 128), F32),
            jax.ShapeDtypeStruct((SUM_ROWS, 8, 128), F32),
            jax.ShapeDtypeStruct((1, RECEPTORS), F32),
        ),
        in_specs=[hbm, hbm, pl.BlockSpec(memory_space=pl.ANY), vmem, vmem],
        out_specs=(vmem, vmem, vmem),
        scratch_shapes=[
            pltpu.SMEM((2, RECEPTORS), jnp.int32),
            pltpu.SMEM((RECEPTORS,), jnp.int32),
            pltpu.SMEM((RECEPTORS,), F32),
            pltpu.SemaphoreType.DMA((3,)),
        ],
        compiler_params=pltpu.CompilerParams(vmem_limit_bytes=VMEM_LIMIT),
    )(in_hbm(slots), in_hbm(offset), misfit_row.reshape(RECEPTORS), blocks, misfit_row)
    piece = (HALF, 8, 128)
    shape = (TILES // 2 + 1, 2, PERIODS, 8, 128)
    gradient = pl.pallas_call(
        scatter_kernel,
        name="scatter",
        out_shape=jax.ShapeDtypeStruct((PERIODS, 2, 128), F32),
        in_specs=[vmem] * 4,
        out_specs=hbm,
        scratch_shapes=[
            pltpu.VMEM((SIDE, 2, PERIODS, 8, 128), F32),
            pltpu.VMEM((4, SIDE, *piece), F32),
            pltpu.VMEM((4, SIDE, *piece), F32),
            pltpu.VMEM((4, 3, *piece), F32),
            pltpu.VMEM((3, *piece), F32),
            pltpu.VMEM((3, *piece), F32),
            pltpu.VMEM((4, 2, *piece), F32),
            pltpu.VMEM((4, 2, *piece), F32),
            pltpu.VMEM((4, 3, *piece), F32),
            pltpu.VMEM((3, *piece), F32),
            pltpu.VMEM((3, *piece), F32),
            pltpu.VMEM((PERIODS, 8, 128), F32),
            pltpu.SemaphoreType.DMA((42,)),
            pltpu.SemaphoreType.DMA((42,)),
            pltpu.SemaphoreType.DMA,
        ],
        compiler_params=pltpu.CompilerParams(collective_id=1, has_side_effects=True, vmem_limit_bytes=VMEM_LIMIT),
    )(total.reshape(shape), second.reshape(shape), prior, lat)
    return gradient, misfit.reshape(RECEPTORS)


def solution(mesh):
    return jax.shard_map(
        shards,
        mesh=mesh,
        in_specs=(
            P(None, "rec", "tile"),
            P("rec", "tile", None, None, None, None),
            P("rec", "tile", None),
            P("rec"),
            P("rec"),
            P("rec"),
            P(),
            P(),
            P(),
            P("tile", None),
        ),
        out_specs=(P(None, "rec", "tile"), P("rec")),
        check_vma=False,
    )
```

```python
import functools

import jax
import jax.numpy as jnp
from jax import lax
from jax.experimental import pallas as pl
from jax.experimental.pallas import tpu as pltpu
from jax.sharding import PartitionSpec as P

MESH = pl.DeviceIdType.MESH
HIGHEST = lax.Precision.HIGHEST
F32 = jnp.float32
VMEM_LIMIT = 28 << 20

SIDE = 4
CORES = 2
PERIODS = 64
HALF = 32
WINDOW = 8
TILES = 8
ROWS = (TILES + 1) * PERIODS
SUM_ROWS = (TILES + 2) * PERIODS
RECEPTORS = 256
STRIPS = 8
GROUP = 8
UNROLL = 4
Z_NEAR = (2, 6, 1, 7)
Z_FAR = (4, 3, 5)
SENT_ROWS = 60 * 8 + 16
FAR_FIRST = (2, 1, 3)
NEAR_FIRST = (1, 3, 2)


def place():
    rec = lax.axis_index("rec")
    return rec // 8, (rec // 2) % SIDE, rec % 2, lax.axis_index("tile")


def rec_of(x, y, c):
    return ((x % SIDE) * SIDE + (y % SIDE)) * CORES + c


def tile_of(x, y):
    return 2 * (x % SIDE) + (y % SIDE) // 2


def pair_of(y, c):
    return pl.multiple_of(4 * ((y % SIDE) % 2) + 2 * c, 2)


def in_hbm(value):
    return pltpu.with_memory_space_constraint(value, pltpu.HBM)


def greet(peers):
    barrier = pltpu.get_barrier_semaphore()
    for peer in peers:
        pl.semaphore_signal(barrier, inc=1, device_id=peer, device_id_type=MESH)
    return barrier


def plane_peers(x, y, c, z):
    peers = [(rec_of(x, y, 1 - c), z)]
    peers += [(rec_of(x + d, y, c), z) for d in (1, 2, 3)]
    peers += [(rec_of(x, y + d, c), z) for d in (1, 2, 3)]
    return peers


def copy_to(src, dst, send, recv, peer):
    return pltpu.make_async_remote_copy(
        src_ref=src, dst_ref=dst, send_sem=send, recv_sem=recv, device_id=peer, device_id_type=MESH
    )


def forward_kernel(
    slots_hbm,
    starts_hbm,
    group_var_hbm,
    dev,
    dev_rows,
    foot,
    observed_hbm,
    group_hbm,
    inv_time_hbm,
    inv_lat_hbm,
    inv_lon_hbm,
    misfit_out,
    prior_out,
    lat_out,
    packed,
    slots,
    starts,
    group_var,
    observed,
    group,
    inv_time,
    inv_lat,
    inv_lon,
    i_sem,
    strip,
    sums,
    field,
    shares,
    own_share,
    send_sem,
    recv_sem,
    near_sem,
    token,
    z_send,
    z_recv,
    s_send,
    s_recv,
    f_sem,
    l_sem,
):
    x, y, c, z = place()
    me = rec_of(x, y, c)
    partner = (rec_of(x, y, 1 - c), z)
    peers = plane_peers(x, y, c, z) + [(me, (z + d) % STRIPS) for d in Z_NEAR]
    barrier = greet(peers)
    load_all = pltpu.make_async_copy(foot.at[:, 0], packed, f_sem)
    load_all.start()
    small = []
    for n, (src, dst) in enumerate((
        (inv_time_hbm, inv_time), (inv_lat_hbm, inv_lat), (slots_hbm, slots), (starts_hbm, starts),
        (group_var_hbm, group_var), (observed_hbm, observed), (group_hbm, group), (inv_lon_hbm, inv_lon),
    )):
        load = pltpu.make_async_copy(src, dst, i_sem.at[n])
        load.start()
        small.append(load)

    def spot(sx, sy, sc, first, count):
        return strip.at[
            pl.ds(pl.multiple_of(PERIODS * (1 + tile_of(sx, sy)) + first, HALF), count), pl.ds(pair_of(sy, sc), 2), :
        ]

    own_local = pltpu.make_async_copy(dev, spot(x, y, c, 0, PERIODS), l_sem.at[0])
    own_local.start()
    own_field = pltpu.make_async_copy(dev_rows, field.at[z], l_sem.at[1])
    own_field.start()
    pl.semaphore_wait(barrier, len(peers))
    for n, d in enumerate((2, STRIPS - 2)):
        pl.semaphore_signal(token.at[n], inc=1, device_id=(me, (z + d) % STRIPS), device_id_type=MESH)

    count = [0]

    def send(src, where, peer):
        n = count[0]
        count[0] += 1
        copy_to(src, where, send_sem, recv_sem.at[n], peer).start()
        return n

    def share_with_partner(src, where):
        copy_to(src, where, send_sem, near_sem, partner).start()

    def arrived(n, where):
        copy_to(where, where, send_sem, recv_sem.at[n], partner).wait_recv()

    first_a, first_b = dev.at[pl.ds(0, HALF)], dev.at[pl.ds(HALF, HALF)]
    in_a, in_b, far_a, far_b = {}, {}, {}, {}
    for d in FAR_FIRST:
        in_a[d] = send(first_a, spot(x, y, c, 0, HALF), (rec_of(x + d, y, c), z))
        in_b[d] = send(first_b, spot(x, y, c, HALF, HALF), (rec_of(x, y + d, c), z))
    for d in FAR_FIRST:
        far_a[0, d] = send(first_a, spot(x, y, c, 0, HALF), (rec_of(x, y + d, c), z))
        far_b[0, d] = send(first_b, spot(x, y, c, HALF, HALF), (rec_of(x + d, y, c), z))
    share_with_partner(dev, spot(x, y, c, 0, PERIODS))

    def send_along(d):
        copy_to(dev_rows, field.at[z], z_send, z_recv, (me, (z + d) % STRIPS)).start()

    for d in Z_NEAR:
        send_along(d)

    strip[pl.ds(0, PERIODS)] = jnp.zeros((PERIODS, 8, 128), F32)
    for load in small:
        load.wait()

    wide = (lax.broadcasted_iota(jnp.int32, (2 * PERIODS, PERIODS), 0) // 2
            == lax.broadcasted_iota(jnp.int32, (2 * PERIODS, PERIODS), 1)).astype(F32)
    time_rows = jnp.dot(wide, inv_time[...], precision=HIGHEST, preferred_element_type=F32)
    time_both = lax.dot_general(time_rows, wide, (((1,), (1,)), ((), ())), precision=HIGHEST, preferred_element_type=F32)
    square = (2 * PERIODS, 2 * PERIODS)
    same = lax.broadcasted_iota(jnp.int32, square, 0) % 2 == lax.broadcasted_iota(jnp.int32, square, 1) % 2
    time_both = jnp.where(same, time_both, 0.0)
    for n in range(2):
        pick = (lax.broadcasted_iota(jnp.int32, (64, 128), 0) == 2 * me + n).astype(F32)
        lat_out[n] = jnp.dot(inv_lat[...], pick, precision=HIGHEST, preferred_element_type=F32)

    for m in range(2):
        pl.semaphore_wait(token.at[m], 1)
    for d in Z_FAR:
        send_along(d)

    for d in NEAR_FIRST:
        here = spot(x - d, y, c, 0, HALF)
        arrived(in_a[d], here)
        for e in FAR_FIRST:
            far_a[d, e] = send(here, here, (rec_of(x, y + e, c), z))
        share_with_partner(here, here)
        here = spot(x, y - d, c, HALF, HALF)
        arrived(in_b[d], here)
        for e in FAR_FIRST:
            far_b[d, e] = send(here, here, (rec_of(x + e, y, c), z))
        share_with_partner(here, here)
    for d in (0, *NEAR_FIRST):
        for e in NEAR_FIRST:
            here = spot(x - d, y - e, c, 0, HALF)
            arrived(far_a[d, e], here)
            share_with_partner(here, here)
            here = spot(x - e, y - d, c, HALF, HALF)
            arrived(far_b[d, e], here)
            share_with_partner(here, here)
    half_strip = strip.at[pl.ds(0, TILES * PERIODS // 2)]
    copy_to(half_strip, half_strip, send_sem, near_sem, partner).wait_recv()
    own_local.wait()
    load_all.wait()

    def group_sums(block, i, carry):
        totals = []
        for u in range(GROUP):
            r = block * 128 + i * GROUP + u
            start = starts[r]
            parts = []
            for k in range(2):
                base = (slots[block, k, i * GROUP + u] + 1) * PERIODS + start
                parts.append(strip[pl.ds(base, WINDOW)] * packed[r, k].astype(F32))
            totals.append(jnp.sum(parts[0] + parts[1], axis=0))
        sums[pl.ds(pl.multiple_of(block * 128 + i * GROUP, GROUP), GROUP), :] = jnp.sum(jnp.stack(totals), axis=1)
        return carry

    for block in range(2):
        lax.fori_loop(0, 128 // GROUP, functools.partial(group_sums, block), 0)
    share = lax.dot_general(
        jnp.ones((8, 128), F32), sums[...], (((1,), (1,)), ((), ())), precision=HIGHEST, preferred_element_type=F32
    )
    own_share[...] = share
    for d in Z_FAR + Z_NEAR:
        copy_to(
            own_share.at[pl.ds(0, 1), :], shares.at[pl.ds(z, 1), :], s_send, s_recv, (me, (z + d) % STRIPS)
        ).start()
    mine = pltpu.make_async_copy(own_share.at[pl.ds(0, 1), :], shares.at[pl.ds(z, 1), :], l_sem.at[2])
    mine.start()

    own_field.wait()
    others = field.at[pl.ds(0, STRIPS - 1)]
    copy_to(others, others, z_send, z_recv, partner).wait()
    lon_done = jnp.zeros((2 * PERIODS, 128), F32)
    for s in range(STRIPS):
        lon_done += lax.dot_general(
            field[s], inv_lon[:, s * 128 : (s + 1) * 128], (((1,), (1,)), ((), ())),
            precision=HIGHEST, preferred_element_type=F32,
        )
    prior_out[...] = jnp.dot(time_both, lon_done, precision=HIGHEST, preferred_element_type=F32)

    mine.wait()
    sent = strip.at[pl.ds(0, SENT_ROWS)]
    copy_to(sent, sent, send_sem, near_sem, partner).wait_send()
    others = shares.at[pl.ds(0, STRIPS - 1), :]
    copy_to(others, others, s_send, s_recv, partner).wait()
    predicted = jnp.sum(shares[...], axis=0, keepdims=True)
    variance = jnp.zeros((1, RECEPTORS), F32)
    for g in range(4):
        variance += jnp.where(group[...] == g, group_var[g], 0.0)
    misfit_out[...] = (predicted - observed[...]) / variance


def adjoint_kernel(
    slots_hbm, starts_hbm, misfit_hbm, blocks, misfit_row, total, second, misfit_out, slots, starts, misfit, i_sem
):
    small = []
    for n, (src, dst) in enumerate(((slots_hbm, slots), (starts_hbm, starts), (misfit_hbm, misfit))):
        load = pltpu.make_async_copy(src, dst, i_sem.at[n])
        load.start()
        small.append(load)
    misfit_out[...] = misfit_row[...]

    def clear(i, carry):
        rows = pl.ds(pl.multiple_of(i * 16, 16), 16)
        total[rows] = jnp.zeros((16, 8, 128), F32)
        second[rows] = jnp.zeros((16, 8, 128), F32)
        return carry

    lax.fori_loop(0, SUM_ROWS // 16, clear, 0)
    for load in small:
        load.wait()

    def pair(block, i, carry):
        held = []
        for u, into in ((0, total), (1, second)):
            r = block * 128 + 2 * i + u
            start = starts[r]
            weight = misfit[r]
            for k in range(2):
                rows = pl.ds((slots[block, k, 2 * i + u] + 2) * PERIODS + start, WINDOW)
                held.append((into, rows, into[rows] + blocks[r, k].astype(F32) * weight))
        for into, rows, value in held:
            into[rows] = value
        return carry

    for block in range(2):
        lax.fori_loop(0, 64, functools.partial(pair, block), 0, unroll=UNROLL)


ORDER = (2, 1, 3, 0)


def scatter_kernel(
    total, second, prior, lat, out, part, a_swap, a_both, a_got, a_sum, a_last, b_swap, b_both, b_got, b_sum, b_last,
    done, send_sem, recv_sem,
):
    x, y, c, z = place()
    partner = (rec_of(x, y, 1 - c), z)
    peers = plane_peers(x, y, c, z)
    barrier = greet(peers)

    def one_period(p, carry):
        first = jnp.broadcast_to(prior[pl.ds(2 * p, 1), :], (8, 128))
        other = jnp.broadcast_to(prior[pl.ds(2 * p + 1, 1), :], (8, 128))
        for t in range(TILES):
            rows = slice(8 * t, 8 * t + 8)
            part[t // 2, t % 2, p] = (
                total[1 + t // 2, t % 2, p] + second[1 + t // 2, t % 2, p]
                + (lat[0, rows, :] * first + lat[1, rows, :] * other)
            )
        return carry

    lax.fori_loop(0, PERIODS, one_period, 0)
    pl.semaphore_wait(barrier, len(peers))

    first_half, second_half = pl.ds(0, HALF), pl.ds(HALF, HALF)
    def send(n, src, dst, peer):
        copy_to(src, dst, send_sem, recv_sem.at[n], peer).start()

    def arrived(n, where):
        copy_to(where, where, send_sem, recv_sem.at[n], partner).wait_recv()

    def pair_rows(sy, sc):
        return pl.ds(pair_of(sy, sc), 2)

    def half_of(sy):
        return (sy % SIDE) // 2

    mine = pair_rows(y, c)
    for e in ORDER:
        theirs = pair_rows(y + e, 1 - c)
        send(e, part.at[:, half_of(y + e), first_half, theirs, :], a_swap.at[e, :, :, theirs, :], partner)
        for h in range(2):
            rows = pl.ds(pl.multiple_of(4 * h + 2 * (1 - c), 2), 2)
            send(4 + e, part.at[(x + e) % SIDE, :, second_half, rows, :], b_swap.at[e, :, :, rows, :], partner)
    for e in ORDER:
        rows = pair_rows(y + e, c)
        arrived(e, a_swap.at[e, :, :, rows, :])
        for s in range(SIDE):
            a_both[e, s] = part[s, half_of(y + e), first_half] + a_swap[e, s]
        for d in FAR_FIRST:
            send(
                8 + e, a_both.at[e, (x + d) % SIDE, :, rows, :], a_got.at[e, d - 1, :, rows, :], (rec_of(x + d, y, c), z)
            )
        both_rows = b_swap.at[e, :, :, pl.ds(0, 4), :]
        arrived(4 + e, both_rows)
        for th in range(2):
            b_both[e, th] = part[(x + e) % SIDE, th, second_half] + b_swap[e, th]
        for d in FAR_FIRST:
            send(
                12 + e,
                b_both.at[e, half_of(y + d), :, pair_rows(y + d, c), :],
                b_got.at[e, d - 1, :, pair_rows(y + d, c), :],
                (rec_of(x, y + d, c), z),
            )
    for e in ORDER:
        rows = pair_rows(y + e, c)
        arrived(8 + e, a_got.at[e, :, :, rows, :])
        a_total = a_both[e, x] + a_got[e, 0] + a_got[e, 1] + a_got[e, 2]
        if e:
            a_sum[e - 1] = a_total
            send(16, a_sum.at[e - 1, :, rows, :], a_last.at[e - 1, :, rows, :], (rec_of(x, y + e, c), z))
        else:
            done[first_half] = a_total
        arrived(12 + e, b_got.at[e, :, :, mine, :])
        b_total = b_both[e, half_of(y)] + b_got[e, 0] + b_got[e, 1] + b_got[e, 2]
        if e:
            b_sum[e - 1] = b_total
            send(17, b_sum.at[e - 1, :, mine, :], b_last.at[e - 1, :, mine, :], (rec_of(x + e, y, c), z))
        else:
            done[second_half] = b_total
    sent = total.at[pl.ds(0, 4), :, pl.ds(0, 62), :, :]
    copy_to(sent, sent, send_sem, recv_sem.at[0], partner).wait_send()
    arrived(16, a_last.at[:, :, mine, :])
    out[first_half] = (
        done[first_half, mine, :] + a_last[0, :, mine, :] + a_last[1, :, mine, :] + a_last[2, :, mine, :]
    )
    arrived(17, b_last.at[:, :, mine, :])
    out[second_half] = (
        done[second_half, mine, :] + b_last[0, :, mine, :] + b_last[1, :, mine, :] + b_last[2, :, mine, :]
    )


def shards(
    deviation, footprint, tile_list, offset, observed, obs_group, group_var, inv_time, inv_lat, inv_lon
):
    vmem = pl.BlockSpec(memory_space=pltpu.VMEM)
    hbm = pl.BlockSpec(memory_space=pltpu.HBM)
    slots = jnp.transpose(tile_list.reshape(2, 128, 2), (0, 2, 1))
    misfit_row, prior, lat, packed = pl.pallas_call(
        forward_kernel,
        name="forward",
        out_shape=(
            jax.ShapeDtypeStruct((1, RECEPTORS), F32),
            jax.ShapeDtypeStruct((2 * PERIODS, 128), F32),
            jax.ShapeDtypeStruct((2, 64, 128), F32),
            jax.ShapeDtypeStruct((RECEPTORS, 2, WINDOW, 8, 128), jnp.bfloat16),
        ),
        in_specs=[hbm] * 11,
        out_specs=(vmem, vmem, vmem, vmem),
        scratch_shapes=[
            pltpu.SMEM((2, 2, 128), jnp.int32),
            pltpu.SMEM((RECEPTORS,), jnp.int32),
            pltpu.SMEM((4,), F32),
            pltpu.VMEM((1, RECEPTORS), F32),
            pltpu.VMEM((1, RECEPTORS), jnp.int32),
            pltpu.VMEM((PERIODS, PERIODS), F32),
            pltpu.VMEM((64, 64), F32),
            pltpu.VMEM((128, 1024), F32),
            pltpu.SemaphoreType.DMA((8,)),
            pltpu.VMEM((ROWS, 8, 128), F32),
            pltpu.VMEM((RECEPTORS, 128), F32),
            pltpu.VMEM((STRIPS, 2 * PERIODS, 128), F32),
            pltpu.VMEM((STRIPS, RECEPTORS), F32),
            pltpu.VMEM((8, RECEPTORS), F32),
            pltpu.SemaphoreType.DMA,
            pltpu.SemaphoreType.DMA((30,)),
            pltpu.SemaphoreType.DMA,
            pltpu.SemaphoreType.REGULAR((2,)),
            pltpu.SemaphoreType.DMA,
            pltpu.SemaphoreType.DMA,
            pltpu.SemaphoreType.DMA,
            pltpu.SemaphoreType.DMA,
            pltpu.SemaphoreType.DMA,
            pltpu.SemaphoreType.DMA((3,)),
        ],
        compiler_params=pltpu.CompilerParams(collective_id=0, has_side_effects=True, vmem_limit_bytes=VMEM_LIMIT),
    )(
        *map(in_hbm, (
            slots,
            offset,
            group_var,
            deviation,
            deviation.reshape(2 * PERIODS, 128),
            footprint,
            observed.reshape(1, RECEPTORS),
            obs_group.reshape(1, RECEPTORS),
            inv_time,
            inv_lat,
            inv_lon,
        ))
    )
    total, second, misfit = pl.pallas_call(
        adjoint_kernel,
        name="adjoint",
        out_shape=(
            jax.ShapeDtypeStruct((SUM_ROWS, 8, 128), F32),
            jax.ShapeDtypeStruct((SUM_ROWS, 8, 128), F32),
            jax.ShapeDtypeStruct((1, RECEPTORS), F32),
        ),
        in_specs=[hbm, hbm, pl.BlockSpec(memory_space=pl.ANY), vmem, vmem],
        out_specs=(vmem, vmem, vmem),
        scratch_shapes=[
            pltpu.SMEM((2, 2, 128), jnp.int32),
            pltpu.SMEM((RECEPTORS,), jnp.int32),
            pltpu.SMEM((RECEPTORS,), F32),
            pltpu.SemaphoreType.DMA((3,)),
        ],
        compiler_params=pltpu.CompilerParams(vmem_limit_bytes=VMEM_LIMIT),
    )(in_hbm(slots), in_hbm(offset), misfit_row.reshape(RECEPTORS), packed, misfit_row)
    piece = (HALF, 8, 128)
    shape = (TILES // 2 + 1, 2, PERIODS, 8, 128)
    gradient = pl.pallas_call(
        scatter_kernel,
        name="scatter",
        out_shape=jax.ShapeDtypeStruct((PERIODS, 2, 128), F32),
        in_specs=[vmem] * 4,
        out_specs=vmem,
        scratch_shapes=[
            pltpu.VMEM((SIDE, 2, PERIODS, 8, 128), F32),
            pltpu.VMEM((4, SIDE, *piece), F32),
            pltpu.VMEM((4, SIDE, *piece), F32),
            pltpu.VMEM((4, 3, *piece), F32),
            pltpu.VMEM((3, *piece), F32),
            pltpu.VMEM((3, *piece), F32),
            pltpu.VMEM((4, 2, *piece), F32),
            pltpu.VMEM((4, 2, *piece), F32),
            pltpu.VMEM((4, 3, *piece), F32),
            pltpu.VMEM((3, *piece), F32),
            pltpu.VMEM((3, *piece), F32),
            pltpu.VMEM((PERIODS, 8, 128), F32),
            pltpu.SemaphoreType.DMA,
            pltpu.SemaphoreType.DMA((18,)),
        ],
        compiler_params=pltpu.CompilerParams(collective_id=1, has_side_effects=True, vmem_limit_bytes=VMEM_LIMIT),
    )(total.reshape(shape), second.reshape(shape), prior, lat)
    return gradient, misfit.reshape(RECEPTORS)


def solution(mesh):
    return jax.shard_map(
        shards,
        mesh=mesh,
        in_specs=(
            P(None, "rec", "tile"),
            P("rec", "tile", None, None, None, None),
            P("rec", "tile", None),
            P("rec"),
            P("rec"),
            P("rec"),
            P(),
            P(),
            P(),
            P("tile", None),
        ),
        out_specs=(P(None, "rec", "tile"), P("rec")),
        check_vma=False,
    )
```

```python
import functools

import jax
import jax.numpy as jnp
from jax import lax
from jax.experimental import pallas as pl
from jax.experimental.pallas import tpu as pltpu
from jax.sharding import PartitionSpec as P

MESH = pl.DeviceIdType.MESH
HIGHEST = lax.Precision.HIGHEST
F32 = jnp.float32
VMEM_LIMIT = 28 << 20

SIDE = 4
CORES = 2
PERIODS = 64
HALF = 32
WINDOW = 8
TILES = 8
ROWS = (TILES + 1) * PERIODS
SUM_ROWS = (TILES + 2) * PERIODS
RECEPTORS = 256
STRIPS = 8
GROUP = 8
UNROLL = 8
Z_NEAR = (2, 6, 1, 7)
Z_FAR = (4, 3, 5)
SENT_ROWS = 60 * 8 + 16
FAR_FIRST = (2, 1, 3)
NEAR_FIRST = (1, 3, 2)


def place():
    rec = lax.axis_index("rec")
    return rec // 8, (rec // 2) % SIDE, rec % 2, lax.axis_index("tile")


def rec_of(x, y, c):
    return ((x % SIDE) * SIDE + (y % SIDE)) * CORES + c


def tile_of(x, y):
    return 2 * (x % SIDE) + (y % SIDE) // 2


def pair_of(y, c):
    return pl.multiple_of(4 * ((y % SIDE) % 2) + 2 * c, 2)


def in_hbm(value):
    return pltpu.with_memory_space_constraint(value, pltpu.HBM)


def greet(peers):
    barrier = pltpu.get_barrier_semaphore()
    for peer in peers:
        pl.semaphore_signal(barrier, inc=1, device_id=peer, device_id_type=MESH)
    return barrier


def plane_peers(x, y, c, z):
    peers = [(rec_of(x, y, 1 - c), z)]
    peers += [(rec_of(x + d, y, c), z) for d in (1, 2, 3)]
    peers += [(rec_of(x, y + d, c), z) for d in (1, 2, 3)]
    return peers


def copy_to(src, dst, send, recv, peer):
    return pltpu.make_async_remote_copy(
        src_ref=src, dst_ref=dst, send_sem=send, recv_sem=recv, device_id=peer, device_id_type=MESH
    )


def forward_kernel(
    slots_hbm,
    starts_hbm,
    group_var_hbm,
    dev,
    dev_rows,
    foot,
    observed_hbm,
    group_hbm,
    inv_time_hbm,
    inv_lat_hbm,
    inv_lon_hbm,
    misfit_out,
    prior_out,
    lat_out,
    packed,
    clear_one,
    clear_two,
    slots_out,
    starts_out,
    slots,
    starts,
    group_var,
    observed,
    group,
    inv_time,
    inv_lat,
    inv_lon,
    i_sem,
    firsts,
    blocks,
    strip,
    sums,
    field,
    shares,
    own_share,
    send_sem,
    recv_sem,
    near_sem,
    token,
    z_send,
    z_recv,
    s_send,
    s_recv,
    f_sem,
    l_sem,
):
    x, y, c, z = place()
    me = rec_of(x, y, c)
    partner = (rec_of(x, y, 1 - c), z)
    peers = plane_peers(x, y, c, z) + [(me, (z + d) % STRIPS) for d in Z_NEAR]
    barrier = greet(peers)
    def spot(sx, sy, sc, first, count):
        return strip.at[
            pl.ds(pl.multiple_of(PERIODS * (1 + tile_of(sx, sy)) + first, HALF), count), pl.ds(pair_of(sy, sc), 2), :
        ]

    own_local = pltpu.make_async_copy(dev, spot(x, y, c, 0, PERIODS), l_sem.at[0])
    own_local.start()
    load_all = pltpu.make_async_copy(foot.at[:, 0], packed, f_sem)
    load_all.start()
    small = []
    for n, (src, dst) in enumerate((
        (inv_time_hbm, inv_time), (inv_lat_hbm, inv_lat), (slots_hbm, slots), (starts_hbm, starts),
        (group_var_hbm, group_var), (observed_hbm, observed), (group_hbm, group), (inv_lon_hbm, inv_lon),
        (slots_hbm, slots_out), (starts_hbm, starts_out),
    )):
        load = pltpu.make_async_copy(src, dst, i_sem.at[n])
        load.start()
        small.append(load)

    own_field = pltpu.make_async_copy(dev_rows, field.at[z], l_sem.at[1])
    own_field.start()
    own_local.wait()
    pl.semaphore_wait(barrier, len(peers))
    for n, d in enumerate((2, STRIPS - 2)):
        pl.semaphore_signal(token.at[n], inc=1, device_id=(me, (z + d) % STRIPS), device_id_type=MESH)

    count = [0]

    def send(src, where, peer):
        n = count[0]
        count[0] += 1
        copy_to(src, where, send_sem, recv_sem.at[n], peer).start()
        return n

    def share_with_partner(src, where):
        copy_to(src, where, send_sem, near_sem, partner).start()

    def arrived(n, where):
        copy_to(where, where, send_sem, recv_sem.at[n], partner).wait_recv()

    first_a, first_b = spot(x, y, c, 0, HALF), spot(x, y, c, HALF, HALF)
    first_both = spot(x, y, c, 0, PERIODS)
    in_a, in_b, far_a, far_b = {}, {}, {}, {}
    for d in FAR_FIRST:
        in_a[d] = send(first_a, spot(x, y, c, 0, HALF), (rec_of(x + d, y, c), z))
        in_b[d] = send(first_b, spot(x, y, c, HALF, HALF), (rec_of(x, y + d, c), z))
    for d in FAR_FIRST:
        far_a[0, d] = send(first_a, spot(x, y, c, 0, HALF), (rec_of(x, y + d, c), z))
        far_b[0, d] = send(first_b, spot(x, y, c, HALF, HALF), (rec_of(x + d, y, c), z))
    share_with_partner(first_both, first_both)

    def send_along(d):
        copy_to(dev_rows, field.at[z], z_send, z_recv, (me, (z + d) % STRIPS)).start()

    for d in Z_NEAR:
        send_along(d)

    strip[pl.ds(0, PERIODS)] = jnp.zeros((PERIODS, 8, 128), F32)
    for load in small:
        load.wait()

    wide = (lax.broadcasted_iota(jnp.int32, (2 * PERIODS, PERIODS), 0) // 2
            == lax.broadcasted_iota(jnp.int32, (2 * PERIODS, PERIODS), 1)).astype(F32)
    time_rows = jnp.dot(wide, inv_time[...], precision=HIGHEST, preferred_element_type=F32)
    time_both = lax.dot_general(time_rows, wide, (((1,), (1,)), ((), ())), precision=HIGHEST, preferred_element_type=F32)
    square = (2 * PERIODS, 2 * PERIODS)
    same = lax.broadcasted_iota(jnp.int32, square, 0) % 2 == lax.broadcasted_iota(jnp.int32, square, 1) % 2
    time_both = jnp.where(same, time_both, 0.0)
    for n in range(2):
        pick = (lax.broadcasted_iota(jnp.int32, (64, 128), 0) == 2 * me + n).astype(F32)
        lat_out[n] = jnp.dot(inv_lat[...], pick, precision=HIGHEST, preferred_element_type=F32)

    for m in range(2):
        pl.semaphore_wait(token.at[m], 1)
    for d in Z_FAR:
        send_along(d)

    for d in NEAR_FIRST:
        here = spot(x - d, y, c, 0, HALF)
        arrived(in_a[d], here)
        for e in FAR_FIRST:
            far_a[d, e] = send(here, here, (rec_of(x, y + e, c), z))
        share_with_partner(here, here)
        here = spot(x, y - d, c, HALF, HALF)
        arrived(in_b[d], here)
        for e in FAR_FIRST:
            far_b[d, e] = send(here, here, (rec_of(x + e, y, c), z))
        share_with_partner(here, here)

    def clear(i, carry):
        rows = pl.ds(pl.multiple_of(i * 16, 16), 16)
        clear_one[rows] = jnp.zeros((16, 8, 128), F32)
        clear_two[rows] = jnp.zeros((16, 8, 128), F32)
        return carry

    lax.fori_loop(0, SUM_ROWS // 16, clear, 0)
    load_all.wait()

    def widen(block, i, carry):
        r = block * 128 + i
        blocks[r] = packed[r].astype(F32)
        for k in range(2):
            firsts[2 * r + k] = (slots[block, k, i] + 1) * PERIODS + starts[r]
        return carry

    for block in range(2):
        lax.fori_loop(0, 128, functools.partial(widen, block), 0, unroll=4)
    for d in (0, *NEAR_FIRST):
        for e in NEAR_FIRST:
            here = spot(x - d, y - e, c, 0, HALF)
            arrived(far_a[d, e], here)
            share_with_partner(here, here)
            here = spot(x - e, y - d, c, HALF, HALF)
            arrived(far_b[d, e], here)
            share_with_partner(here, here)
    half_strip = strip.at[pl.ds(0, TILES * PERIODS // 2)]
    copy_to(half_strip, half_strip, send_sem, near_sem, partner).wait_recv()

    def group_sums(block, i, carry):
        totals = []
        for u in range(GROUP):
            r = block * 128 + i * GROUP + u
            parts = []
            for k in range(2):
                base = firsts[2 * r + k]
                parts.append(strip[pl.ds(base, WINDOW)] * blocks[r, k])
            totals.append(jnp.sum(parts[0] + parts[1], axis=0))
        sums[pl.ds(pl.multiple_of(block * 128 + i * GROUP, GROUP), GROUP), :] = jnp.sum(jnp.stack(totals), axis=1)
        return carry

    for block in range(2):
        lax.fori_loop(0, 128 // GROUP, functools.partial(group_sums, block), 0, unroll=2)
    share = lax.dot_general(
        jnp.ones((8, 128), F32), sums[...], (((1,), (1,)), ((), ())), precision=HIGHEST, preferred_element_type=F32
    )
    own_share[...] = share
    for d in Z_FAR + Z_NEAR:
        copy_to(
            own_share.at[pl.ds(0, 1), :], shares.at[pl.ds(z, 1), :], s_send, s_recv, (me, (z + d) % STRIPS)
        ).start()
    mine = pltpu.make_async_copy(own_share.at[pl.ds(0, 1), :], shares.at[pl.ds(z, 1), :], l_sem.at[2])
    mine.start()

    own_field.wait()
    others = field.at[pl.ds(0, STRIPS - 1)]
    copy_to(others, others, z_send, z_recv, partner).wait()
    lon_done = jnp.zeros((2 * PERIODS, 128), F32)
    for s in range(STRIPS):
        lon_done += lax.dot_general(
            field[s], inv_lon[:, s * 128 : (s + 1) * 128], (((1,), (1,)), ((), ())),
            precision=HIGHEST, preferred_element_type=F32,
        )
    prior_out[...] = jnp.dot(time_both, lon_done, precision=HIGHEST, preferred_element_type=F32)

    mine.wait()
    sent = strip.at[pl.ds(0, SENT_ROWS)]
    copy_to(sent, sent, send_sem, near_sem, partner).wait_send()
    others = shares.at[pl.ds(0, STRIPS - 1), :]
    copy_to(others, others, s_send, s_recv, partner).wait()
    predicted = jnp.sum(shares[...], axis=0, keepdims=True)
    variance = jnp.zeros((1, RECEPTORS), F32)
    for g in range(4):
        variance += jnp.where(group[...] == g, group_var[g], 0.0)
    misfit_out[...] = (predicted - observed[...]) / variance


def adjoint_kernel(
    slots_hbm, starts_hbm, misfit_hbm, blocks, misfit_row, clear_one, clear_two, total, second, misfit_out, slots, starts, misfit, i_sem
):
    small = []
    for n, (src, dst) in enumerate(((slots_hbm, slots), (starts_hbm, starts), (misfit_hbm, misfit))):
        load = pltpu.make_async_copy(src, dst, i_sem.at[n])
        load.start()
        small.append(load)
    result = pltpu.make_async_copy(misfit_row, misfit_out, i_sem.at[3])
    result.start()

    for load in small:
        load.wait()

    def pair(block, i, carry):
        held = []
        for u, into in ((0, total), (1, second)):
            r = block * 128 + 2 * i + u
            start = starts[r]
            weight = misfit[r]
            for k in range(2):
                rows = pl.ds((slots[block, k, 2 * i + u] + 2) * PERIODS + start, WINDOW)
                held.append((into, rows, into[rows] + blocks[r, k].astype(F32) * weight))
        for into, rows, value in held:
            into[rows] = value
        return carry

    for block in range(2):
        lax.fori_loop(0, 64, functools.partial(pair, block), 0, unroll=UNROLL)
    result.wait()


ORDER = (2, 1, 3, 0)


def scatter_kernel(
    total, second, prior, lat, out, part, a_swap, a_both, a_got, a_sum, a_last, b_swap, b_both, b_got, b_sum, b_last,
    done, send_sem, recv_sem,
):
    x, y, c, z = place()
    partner = (rec_of(x, y, 1 - c), z)
    peers = plane_peers(x, y, c, z)
    barrier = greet(peers)

    def one_period(p, carry):
        first = jnp.broadcast_to(prior[pl.ds(2 * p, 1), :], (8, 128))
        other = jnp.broadcast_to(prior[pl.ds(2 * p + 1, 1), :], (8, 128))
        for t in range(TILES):
            rows = slice(8 * t, 8 * t + 8)
            part[t // 2, t % 2, p] = (
                total[1 + t // 2, t % 2, p] + second[1 + t // 2, t % 2, p]
                + (lat[0, rows, :] * first + lat[1, rows, :] * other)
            )
        return carry

    lax.fori_loop(0, PERIODS, one_period, 0)
    pl.semaphore_wait(barrier, len(peers))

    first_half, second_half = pl.ds(0, HALF), pl.ds(HALF, HALF)
    def send(n, src, dst, peer):
        copy_to(src, dst, send_sem, recv_sem.at[n], peer).start()

    def arrived(n, where):
        copy_to(where, where, send_sem, recv_sem.at[n], partner).wait_recv()

    def pair_rows(sy, sc):
        return pl.ds(pair_of(sy, sc), 2)

    def half_of(sy):
        return (sy % SIDE) // 2

    mine = pair_rows(y, c)
    for e in ORDER:
        theirs = pair_rows(y + e, 1 - c)
        send(e, part.at[:, half_of(y + e), first_half, theirs, :], a_swap.at[e, :, :, theirs, :], partner)
        for h in range(2):
            rows = pl.ds(pl.multiple_of(4 * h + 2 * (1 - c), 2), 2)
            send(4 + e, part.at[(x + e) % SIDE, :, second_half, rows, :], b_swap.at[e, :, :, rows, :], partner)
    for e in ORDER:
        rows = pair_rows(y + e, c)
        arrived(e, a_swap.at[e, :, :, rows, :])
        for s in range(SIDE):
            a_both[e, s] = part[s, half_of(y + e), first_half] + a_swap[e, s]
        for d in FAR_FIRST:
            send(
                8 + e, a_both.at[e, (x + d) % SIDE, :, rows, :], a_got.at[e, d - 1, :, rows, :], (rec_of(x + d, y, c), z)
            )
        both_rows = b_swap.at[e, :, :, pl.ds(0, 4), :]
        arrived(4 + e, both_rows)
        for th in range(2):
            b_both[e, th] = part[(x + e) % SIDE, th, second_half] + b_swap[e, th]
        for d in FAR_FIRST:
            send(
                12 + e,
                b_both.at[e, half_of(y + d), :, pair_rows(y + d, c), :],
                b_got.at[e, d - 1, :, pair_rows(y + d, c), :],
                (rec_of(x, y + d, c), z),
            )
    for e in ORDER:
        rows = pair_rows(y + e, c)
        arrived(8 + e, a_got.at[e, :, :, rows, :])
        a_total = a_both[e, x] + a_got[e, 0] + a_got[e, 1] + a_got[e, 2]
        if e:
            a_sum[e - 1] = a_total
            send(16, a_sum.at[e - 1, :, rows, :], a_last.at[e - 1, :, rows, :], (rec_of(x, y + e, c), z))
        else:
            done[first_half] = a_total
        arrived(12 + e, b_got.at[e, :, :, mine, :])
        b_total = b_both[e, half_of(y)] + b_got[e, 0] + b_got[e, 1] + b_got[e, 2]
        if e:
            b_sum[e - 1] = b_total
            send(17, b_sum.at[e - 1, :, mine, :], b_last.at[e - 1, :, mine, :], (rec_of(x + e, y, c), z))
        else:
            done[second_half] = b_total
    sent = total.at[pl.ds(0, 4), :, pl.ds(0, 62), :, :]
    copy_to(sent, sent, send_sem, recv_sem.at[0], partner).wait_send()
    arrived(16, a_last.at[:, :, mine, :])
    out[first_half] = (
        done[first_half, mine, :] + a_last[0, :, mine, :] + a_last[1, :, mine, :] + a_last[2, :, mine, :]
    )
    arrived(17, b_last.at[:, :, mine, :])
    out[second_half] = (
        done[second_half, mine, :] + b_last[0, :, mine, :] + b_last[1, :, mine, :] + b_last[2, :, mine, :]
    )


def shards(
    deviation, footprint, tile_list, offset, observed, obs_group, group_var, inv_time, inv_lat, inv_lon
):
    vmem = pl.BlockSpec(memory_space=pltpu.VMEM)
    hbm = pl.BlockSpec(memory_space=pltpu.HBM)
    slots = jnp.transpose(tile_list.reshape(2, 128, 2), (0, 2, 1))
    misfit_row, prior, lat, packed, clear_one, clear_two, slots_near, starts_near = pl.pallas_call(
        forward_kernel,
        name="forward",
        out_shape=(
            jax.ShapeDtypeStruct((1, RECEPTORS), F32),
            jax.ShapeDtypeStruct((2 * PERIODS, 128), F32),
            jax.ShapeDtypeStruct((2, 64, 128), F32),
            jax.ShapeDtypeStruct((RECEPTORS, 2, WINDOW, 8, 128), jnp.bfloat16),
            jax.ShapeDtypeStruct((SUM_ROWS, 8, 128), F32),
            jax.ShapeDtypeStruct((SUM_ROWS, 8, 128), F32),
            jax.ShapeDtypeStruct((2, 2, 128), jnp.int32),
            jax.ShapeDtypeStruct((RECEPTORS,), jnp.int32),
        ),
        in_specs=[hbm] * 11,
        out_specs=(vmem,) * 8,
        scratch_shapes=[
            pltpu.SMEM((2, 2, 128), jnp.int32),
            pltpu.SMEM((RECEPTORS,), jnp.int32),
            pltpu.SMEM((4,), F32),
            pltpu.VMEM((1, RECEPTORS), F32),
            pltpu.VMEM((1, RECEPTORS), jnp.int32),
            pltpu.VMEM((PERIODS, PERIODS), F32),
            pltpu.VMEM((64, 64), F32),
            pltpu.VMEM((128, 1024), F32),
            pltpu.SemaphoreType.DMA((10,)),
            pltpu.SMEM((2 * RECEPTORS,), jnp.int32),
            pltpu.VMEM((RECEPTORS, 2, WINDOW, 8, 128), F32),
            pltpu.VMEM((ROWS, 8, 128), F32),
            pltpu.VMEM((RECEPTORS, 128), F32),
            pltpu.VMEM((STRIPS, 2 * PERIODS, 128), F32),
            pltpu.VMEM((STRIPS, RECEPTORS), F32),
            pltpu.VMEM((8, RECEPTORS), F32),
            pltpu.SemaphoreType.DMA,
            pltpu.SemaphoreType.DMA((30,)),
            pltpu.SemaphoreType.DMA,
            pltpu.SemaphoreType.REGULAR((2,)),
            pltpu.SemaphoreType.DMA,
            pltpu.SemaphoreType.DMA,
            pltpu.SemaphoreType.DMA,
            pltpu.SemaphoreType.DMA,
            pltpu.SemaphoreType.DMA,
            pltpu.SemaphoreType.DMA((3,)),
        ],
        compiler_params=pltpu.CompilerParams(collective_id=0, has_side_effects=True, vmem_limit_bytes=VMEM_LIMIT),
    )(
        *map(in_hbm, (
            slots,
            offset,
            group_var,
            deviation,
            deviation.reshape(2 * PERIODS, 128),
            footprint,
            observed.reshape(1, RECEPTORS),
            obs_group.reshape(1, RECEPTORS),
            inv_time,
            inv_lat,
            inv_lon,
        ))
    )
    total, second, misfit = pl.pallas_call(
        adjoint_kernel,
        name="adjoint",
        out_shape=(
            jax.ShapeDtypeStruct((SUM_ROWS, 8, 128), F32),
            jax.ShapeDtypeStruct((SUM_ROWS, 8, 128), F32),
            jax.ShapeDtypeStruct((1, RECEPTORS), F32),
        ),
        in_specs=[pl.BlockSpec(memory_space=pl.ANY)] * 3 + [vmem] * 4,
        input_output_aliases={5: 0, 6: 1},
        out_specs=(vmem, vmem, hbm),
        scratch_shapes=[
            pltpu.SMEM((2, 2, 128), jnp.int32),
            pltpu.SMEM((RECEPTORS,), jnp.int32),
            pltpu.SMEM((RECEPTORS,), F32),
            pltpu.SemaphoreType.DMA((4,)),
        ],
        compiler_params=pltpu.CompilerParams(vmem_limit_bytes=VMEM_LIMIT),
    )(slots_near, starts_near, misfit_row.reshape(RECEPTORS), packed, misfit_row, clear_one, clear_two)
    piece = (HALF, 8, 128)
    shape = (TILES // 2 + 1, 2, PERIODS, 8, 128)
    gradient = pl.pallas_call(
        scatter_kernel,
        name="scatter",
        out_shape=jax.ShapeDtypeStruct((PERIODS, 2, 128), F32),
        in_specs=[vmem] * 4,
        out_specs=vmem,
        scratch_shapes=[
            pltpu.VMEM((SIDE, 2, PERIODS, 8, 128), F32),
            pltpu.VMEM((4, SIDE, *piece), F32),
            pltpu.VMEM((4, SIDE, *piece), F32),
            pltpu.VMEM((4, 3, *piece), F32),
            pltpu.VMEM((3, *piece), F32),
            pltpu.VMEM((3, *piece), F32),
            pltpu.VMEM((4, 2, *piece), F32),
            pltpu.VMEM((4, 2, *piece), F32),
            pltpu.VMEM((4, 3, *piece), F32),
            pltpu.VMEM((3, *piece), F32),
            pltpu.VMEM((3, *piece), F32),
            pltpu.VMEM((PERIODS, 8, 128), F32),
            pltpu.SemaphoreType.DMA,
            pltpu.SemaphoreType.DMA((18,)),
        ],
        compiler_params=pltpu.CompilerParams(collective_id=1, has_side_effects=True, vmem_limit_bytes=VMEM_LIMIT),
    )(total.reshape(shape), second.reshape(shape), prior, lat)
    return gradient, misfit.reshape(RECEPTORS)


def solution(mesh):
    return jax.shard_map(
        shards,
        mesh=mesh,
        in_specs=(
            P(None, "rec", "tile"),
            P("rec", "tile", None, None, None, None),
            P("rec", "tile", None),
            P("rec"),
            P("rec"),
            P("rec"),
            P(),
            P(),
            P(),
            P("tile", None),
        ),
        out_specs=(P(None, "rec", "tile"), P("rec")),
        check_vma=False,
    )
```

```python
import functools

import jax
import jax.numpy as jnp
from jax import lax
from jax.experimental import pallas as pl
from jax.experimental.pallas import tpu as pltpu
from jax.sharding import PartitionSpec as P

MESH = pl.DeviceIdType.MESH
HIGHEST = lax.Precision.HIGHEST
F32 = jnp.float32
VMEM_LIMIT = 28 << 20

SIDE = 4
CORES = 2
PERIODS = 64
HALF = 32
WINDOW = 8
TILES = 8
ROWS = (TILES + 1) * PERIODS
SUM_ROWS = (TILES + 2) * PERIODS
RECEPTORS = 256
STRIPS = 8
GROUP = 8
UNROLL = 16
Z_NEAR = (2, 6, 1, 7)
Z_FAR = (4, 3, 5)
SENT_ROWS = 60 * 8 + 16
FAR_FIRST = (2, 1, 3)
NEAR_FIRST = (1, 3, 2)


def place():
    rec = lax.axis_index("rec")
    return rec // 8, (rec // 2) % SIDE, rec % 2, lax.axis_index("tile")


def rec_of(x, y, c):
    return ((x % SIDE) * SIDE + (y % SIDE)) * CORES + c


def tile_of(x, y):
    return 2 * (x % SIDE) + (y % SIDE) // 2


def pair_of(y, c):
    return pl.multiple_of(4 * ((y % SIDE) % 2) + 2 * c, 2)


def in_hbm(value):
    return pltpu.with_memory_space_constraint(value, pltpu.HBM)


def greet(peers):
    barrier = pltpu.get_barrier_semaphore()
    for peer in peers:
        pl.semaphore_signal(barrier, inc=1, device_id=peer, device_id_type=MESH)
    return barrier


def plane_peers(x, y, c, z):
    peers = [(rec_of(x, y, 1 - c), z)]
    peers += [(rec_of(x + d, y, c), z) for d in (1, 2, 3)]
    peers += [(rec_of(x, y + d, c), z) for d in (1, 2, 3)]
    return peers


def copy_to(src, dst, send, recv, peer):
    return pltpu.make_async_remote_copy(
        src_ref=src, dst_ref=dst, send_sem=send, recv_sem=recv, device_id=peer, device_id_type=MESH
    )


def forward_kernel(
    slots_hbm,
    starts_hbm,
    group_var_hbm,
    dev,
    dev_rows,
    foot,
    observed_hbm,
    group_hbm,
    inv_time_hbm,
    inv_lat_hbm,
    inv_lon_hbm,
    misfit_out,
    prior_out,
    lat_out,
    packed,
    clear_one,
    clear_two,
    slots_out,
    starts_out,
    slots,
    starts,
    group_var,
    observed,
    group,
    inv_time,
    inv_lat,
    inv_lon,
    i_sem,
    firsts,
    blocks,
    strip,
    sums,
    field,
    shares,
    own_share,
    send_sem,
    recv_sem,
    near_sem,
    token,
    z_send,
    z_recv,
    s_send,
    s_recv,
    f_sem,
    l_sem,
):
    x, y, c, z = place()
    me = rec_of(x, y, c)
    partner = (rec_of(x, y, 1 - c), z)
    peers = plane_peers(x, y, c, z) + [(me, (z + d) % STRIPS) for d in Z_NEAR]
    barrier = greet(peers)
    def spot(sx, sy, sc, first, count):
        return strip.at[
            pl.ds(pl.multiple_of(PERIODS * (1 + tile_of(sx, sy)) + first, HALF), count), pl.ds(pair_of(sy, sc), 2), :
        ]

    own_local = pltpu.make_async_copy(dev, spot(x, y, c, 0, PERIODS), l_sem.at[0])
    own_local.start()
    load_all = pltpu.make_async_copy(foot.at[:, 0], packed, f_sem)
    load_all.start()
    small = []
    for n, (src, dst) in enumerate((
        (inv_time_hbm, inv_time), (inv_lat_hbm, inv_lat), (slots_hbm, slots), (starts_hbm, starts),
        (group_var_hbm, group_var), (observed_hbm, observed), (group_hbm, group), (inv_lon_hbm, inv_lon),
        (slots_hbm, slots_out), (starts_hbm, starts_out),
    )):
        load = pltpu.make_async_copy(src, dst, i_sem.at[n])
        load.start()
        small.append(load)

    own_field = pltpu.make_async_copy(dev_rows, field.at[z], l_sem.at[1])
    own_field.start()
    own_local.wait()
    pl.semaphore_wait(barrier, len(peers))
    for n, d in enumerate((2, STRIPS - 2)):
        pl.semaphore_signal(token.at[n], inc=1, device_id=(me, (z + d) % STRIPS), device_id_type=MESH)

    count = [0]

    def send(src, where, peer):
        n = count[0]
        count[0] += 1
        copy_to(src, where, send_sem, recv_sem.at[n], peer).start()
        return n

    def share_with_partner(src, where):
        copy_to(src, where, send_sem, near_sem, partner).start()

    def arrived(n, where):
        copy_to(where, where, send_sem, recv_sem.at[n], partner).wait_recv()

    first_a, first_b = spot(x, y, c, 0, HALF), spot(x, y, c, HALF, HALF)
    first_both = spot(x, y, c, 0, PERIODS)
    in_a, in_b, far_a, far_b = {}, {}, {}, {}
    for d in FAR_FIRST:
        in_a[d] = send(first_a, spot(x, y, c, 0, HALF), (rec_of(x + d, y, c), z))
        in_b[d] = send(first_b, spot(x, y, c, HALF, HALF), (rec_of(x, y + d, c), z))
    for d in FAR_FIRST:
        far_a[0, d] = send(first_a, spot(x, y, c, 0, HALF), (rec_of(x, y + d, c), z))
        far_b[0, d] = send(first_b, spot(x, y, c, HALF, HALF), (rec_of(x + d, y, c), z))
    share_with_partner(first_both, first_both)

    def send_along(d):
        copy_to(dev_rows, field.at[z], z_send, z_recv, (me, (z + d) % STRIPS)).start()

    for d in Z_NEAR:
        send_along(d)

    strip[pl.ds(0, PERIODS)] = jnp.zeros((PERIODS, 8, 128), F32)
    for load in small:
        load.wait()

    wide = (lax.broadcasted_iota(jnp.int32, (2 * PERIODS, PERIODS), 0) // 2
            == lax.broadcasted_iota(jnp.int32, (2 * PERIODS, PERIODS), 1)).astype(F32)
    time_rows = jnp.dot(wide, inv_time[...], precision=HIGHEST, preferred_element_type=F32)
    time_both = lax.dot_general(time_rows, wide, (((1,), (1,)), ((), ())), precision=HIGHEST, preferred_element_type=F32)
    square = (2 * PERIODS, 2 * PERIODS)
    same = lax.broadcasted_iota(jnp.int32, square, 0) % 2 == lax.broadcasted_iota(jnp.int32, square, 1) % 2
    time_both = jnp.where(same, time_both, 0.0)
    for n in range(2):
        pick = (lax.broadcasted_iota(jnp.int32, (64, 128), 0) == 2 * me + n).astype(F32)
        lat_out[n] = jnp.dot(inv_lat[...], pick, precision=HIGHEST, preferred_element_type=F32)

    for m in range(2):
        pl.semaphore_wait(token.at[m], 1)
    for d in Z_FAR:
        send_along(d)

    for d in NEAR_FIRST:
        here = spot(x - d, y, c, 0, HALF)
        arrived(in_a[d], here)
        for e in FAR_FIRST:
            far_a[d, e] = send(here, here, (rec_of(x, y + e, c), z))
        share_with_partner(here, here)
        here = spot(x, y - d, c, HALF, HALF)
        arrived(in_b[d], here)
        for e in FAR_FIRST:
            far_b[d, e] = send(here, here, (rec_of(x + e, y, c), z))
        share_with_partner(here, here)

    def clear(i, carry):
        rows = pl.ds(pl.multiple_of(i * 16, 16), 16)
        clear_one[rows] = jnp.zeros((16, 8, 128), F32)
        clear_two[rows] = jnp.zeros((16, 8, 128), F32)
        return carry

    lax.fori_loop(0, SUM_ROWS // 16, clear, 0)
    load_all.wait()

    def widen(block, i, carry):
        r = block * 128 + i
        blocks[r] = packed[r].astype(F32)
        for k in range(2):
            firsts[2 * r + k] = (slots[block, k, i] + 1) * PERIODS + starts[r]
        return carry

    for block in range(2):
        lax.fori_loop(0, 128, functools.partial(widen, block), 0, unroll=4)
    for d in (0, *NEAR_FIRST):
        for e in NEAR_FIRST:
            here = spot(x - d, y - e, c, 0, HALF)
            arrived(far_a[d, e], here)
            share_with_partner(here, here)
            here = spot(x - e, y - d, c, HALF, HALF)
            arrived(far_b[d, e], here)
            share_with_partner(here, here)
    half_strip = strip.at[pl.ds(0, TILES * PERIODS // 2)]
    copy_to(half_strip, half_strip, send_sem, near_sem, partner).wait_recv()

    def group_sums(block, i, carry):
        totals = []
        for u in range(GROUP):
            r = block * 128 + i * GROUP + u
            parts = []
            for k in range(2):
                base = firsts[2 * r + k]
                parts.append(strip[pl.ds(base, WINDOW)] * blocks[r, k])
            totals.append(jnp.sum(parts[0] + parts[1], axis=0))
        sums[pl.ds(pl.multiple_of(block * 128 + i * GROUP, GROUP), GROUP), :] = jnp.sum(jnp.stack(totals), axis=1)
        return carry

    for block in range(2):
        lax.fori_loop(0, 128 // GROUP, functools.partial(group_sums, block), 0, unroll=2)
    share = lax.dot_general(
        jnp.ones((8, 128), F32), sums[...], (((1,), (1,)), ((), ())), precision=HIGHEST, preferred_element_type=F32
    )
    own_share[...] = share
    for d in Z_FAR + Z_NEAR:
        copy_to(
            own_share.at[pl.ds(0, 1), :], shares.at[pl.ds(z, 1), :], s_send, s_recv, (me, (z + d) % STRIPS)
        ).start()
    mine = pltpu.make_async_copy(own_share.at[pl.ds(0, 1), :], shares.at[pl.ds(z, 1), :], l_sem.at[2])
    mine.start()

    own_field.wait()
    others = field.at[pl.ds(0, STRIPS - 1)]
    copy_to(others, others, z_send, z_recv, partner).wait()
    lon_done = jnp.zeros((2 * PERIODS, 128), F32)
    for s in range(STRIPS):
        lon_done += lax.dot_general(
            field[s], inv_lon[:, s * 128 : (s + 1) * 128], (((1,), (1,)), ((), ())),
            precision=HIGHEST, preferred_element_type=F32,
        )
    prior_out[...] = jnp.dot(time_both, lon_done, precision=HIGHEST, preferred_element_type=F32)

    mine.wait()
    others = shares.at[pl.ds(0, STRIPS - 1), :]
    copy_to(others, others, s_send, s_recv, partner).wait()
    predicted = jnp.sum(shares[...], axis=0, keepdims=True)
    variance = jnp.zeros((1, RECEPTORS), F32)
    for g in range(4):
        variance += jnp.where(group[...] == g, group_var[g], 0.0)
    misfit_out[...] = (predicted - observed[...]) / variance
    sent = strip.at[pl.ds(0, SENT_ROWS)]
    copy_to(sent, sent, send_sem, near_sem, partner).wait_send()


def adjoint_kernel(
    slots_hbm, starts_hbm, misfit_hbm, blocks, misfit_row, clear_one, clear_two, total, second, misfit_out, slots, starts, misfit, i_sem
):
    small = []
    for n, (src, dst) in enumerate(((slots_hbm, slots), (starts_hbm, starts), (misfit_hbm, misfit))):
        load = pltpu.make_async_copy(src, dst, i_sem.at[n])
        load.start()
        small.append(load)
    result = pltpu.make_async_copy(misfit_row, misfit_out, i_sem.at[3])
    result.start()

    for load in small:
        load.wait()

    def pair(block, i, carry):
        held = []
        for u, into in ((0, total), (1, second)):
            r = block * 128 + 2 * i + u
            start = starts[r]
            weight = misfit[r]
            for k in range(2):
                rows = pl.ds((slots[block, k, 2 * i + u] + 2) * PERIODS + start, WINDOW)
                held.append((into, rows, into[rows] + blocks[r, k].astype(F32) * weight))
        for into, rows, value in held:
            into[rows] = value
        return carry

    for block in range(2):
        lax.fori_loop(0, 64, functools.partial(pair, block), 0, unroll=UNROLL)
    result.wait()


ORDER = (2, 1, 3, 0)


def scatter_kernel(
    total, second, prior, lat, out, part, a_swap, a_both, a_got, a_sum, a_last, b_swap, b_both, b_got, b_sum, b_last,
    done, send_sem, recv_sem,
):
    x, y, c, z = place()
    partner = (rec_of(x, y, 1 - c), z)
    peers = plane_peers(x, y, c, z)
    barrier = greet(peers)

    def one_period(p, carry):
        first = jnp.broadcast_to(prior[pl.ds(2 * p, 1), :], (8, 128))
        other = jnp.broadcast_to(prior[pl.ds(2 * p + 1, 1), :], (8, 128))
        for t in range(TILES):
            rows = slice(8 * t, 8 * t + 8)
            part[t // 2, t % 2, p] = (
                total[1 + t // 2, t % 2, p] + second[1 + t // 2, t % 2, p]
                + (lat[0, rows, :] * first + lat[1, rows, :] * other)
            )
        return carry

    lax.fori_loop(0, PERIODS, one_period, 0)
    pl.semaphore_wait(barrier, len(peers))

    first_half, second_half = pl.ds(0, HALF), pl.ds(HALF, HALF)
    def send(n, src, dst, peer):
        copy_to(src, dst, send_sem, recv_sem.at[n], peer).start()

    def arrived(n, where):
        copy_to(where, where, send_sem, recv_sem.at[n], partner).wait_recv()

    def pair_rows(sy, sc):
        return pl.ds(pair_of(sy, sc), 2)

    def half_of(sy):
        return (sy % SIDE) // 2

    mine = pair_rows(y, c)
    for e in ORDER:
        theirs = pair_rows(y + e, 1 - c)
        send(e, part.at[:, half_of(y + e), first_half, theirs, :], a_swap.at[e, :, :, theirs, :], partner)
        for h in range(2):
            rows = pl.ds(pl.multiple_of(4 * h + 2 * (1 - c), 2), 2)
            send(4 + e, part.at[(x + e) % SIDE, :, second_half, rows, :], b_swap.at[e, :, :, rows, :], partner)
    for e in ORDER:
        rows = pair_rows(y + e, c)
        arrived(e, a_swap.at[e, :, :, rows, :])
        for s in range(SIDE):
            a_both[e, s] = part[s, half_of(y + e), first_half] + a_swap[e, s]
        for d in FAR_FIRST:
            send(
                8 + e, a_both.at[e, (x + d) % SIDE, :, rows, :], a_got.at[e, d - 1, :, rows, :], (rec_of(x + d, y, c), z)
            )
        both_rows = b_swap.at[e, :, :, pl.ds(0, 4), :]
        arrived(4 + e, both_rows)
        for th in range(2):
            b_both[e, th] = part[(x + e) % SIDE, th, second_half] + b_swap[e, th]
        for d in FAR_FIRST:
            send(
                12 + e,
                b_both.at[e, half_of(y + d), :, pair_rows(y + d, c), :],
                b_got.at[e, d - 1, :, pair_rows(y + d, c), :],
                (rec_of(x, y + d, c), z),
            )
    for e in ORDER:
        rows = pair_rows(y + e, c)
        arrived(8 + e, a_got.at[e, :, :, rows, :])
        a_total = a_both[e, x] + a_got[e, 0] + a_got[e, 1] + a_got[e, 2]
        if e:
            a_sum[e - 1] = a_total
            send(16, a_sum.at[e - 1, :, rows, :], a_last.at[e - 1, :, rows, :], (rec_of(x, y + e, c), z))
        else:
            done[first_half] = a_total
        arrived(12 + e, b_got.at[e, :, :, mine, :])
        b_total = b_both[e, half_of(y)] + b_got[e, 0] + b_got[e, 1] + b_got[e, 2]
        if e:
            b_sum[e - 1] = b_total
            send(17, b_sum.at[e - 1, :, mine, :], b_last.at[e - 1, :, mine, :], (rec_of(x + e, y, c), z))
        else:
            done[second_half] = b_total
    arrived(16, a_last.at[:, :, mine, :])
    out[first_half] = (
        done[first_half, mine, :] + a_last[0, :, mine, :] + a_last[1, :, mine, :] + a_last[2, :, mine, :]
    )
    arrived(17, b_last.at[:, :, mine, :])
    out[second_half] = (
        done[second_half, mine, :] + b_last[0, :, mine, :] + b_last[1, :, mine, :] + b_last[2, :, mine, :]
    )
    sent = total.at[pl.ds(0, 4), :, pl.ds(0, 62), :, :]
    copy_to(sent, sent, send_sem, recv_sem.at[0], partner).wait_send()


def shards(
    deviation, footprint, tile_list, offset, observed, obs_group, group_var, inv_time, inv_lat, inv_lon
):
    vmem = pl.BlockSpec(memory_space=pltpu.VMEM)
    hbm = pl.BlockSpec(memory_space=pltpu.HBM)
    slots = jnp.transpose(tile_list.reshape(2, 128, 2), (0, 2, 1))
    misfit_row, prior, lat, packed, clear_one, clear_two, slots_near, starts_near = pl.pallas_call(
        forward_kernel,
        name="forward",
        out_shape=(
            jax.ShapeDtypeStruct((1, RECEPTORS), F32),
            jax.ShapeDtypeStruct((2 * PERIODS, 128), F32),
            jax.ShapeDtypeStruct((2, 64, 128), F32),
            jax.ShapeDtypeStruct((RECEPTORS, 2, WINDOW, 8, 128), jnp.bfloat16),
            jax.ShapeDtypeStruct((SUM_ROWS, 8, 128), F32),
            jax.ShapeDtypeStruct((SUM_ROWS, 8, 128), F32),
            jax.ShapeDtypeStruct((2, 2, 128), jnp.int32),
            jax.ShapeDtypeStruct((RECEPTORS,), jnp.int32),
        ),
        in_specs=[hbm] * 11,
        out_specs=(vmem,) * 8,
        scratch_shapes=[
            pltpu.SMEM((2, 2, 128), jnp.int32),
            pltpu.SMEM((RECEPTORS,), jnp.int32),
            pltpu.SMEM((4,), F32),
            pltpu.VMEM((1, RECEPTORS), F32),
            pltpu.VMEM((1, RECEPTORS), jnp.int32),
            pltpu.VMEM((PERIODS, PERIODS), F32),
            pltpu.VMEM((64, 64), F32),
            pltpu.VMEM((128, 1024), F32),
            pltpu.SemaphoreType.DMA((10,)),
            pltpu.SMEM((2 * RECEPTORS,), jnp.int32),
            pltpu.VMEM((RECEPTORS, 2, WINDOW, 8, 128), F32),
            pltpu.VMEM((ROWS, 8, 128), F32),
            pltpu.VMEM((RECEPTORS, 128), F32),
            pltpu.VMEM((STRIPS, 2 * PERIODS, 128), F32),
            pltpu.VMEM((STRIPS, RECEPTORS), F32),
            pltpu.VMEM((8, RECEPTORS), F32),
            pltpu.SemaphoreType.DMA,
            pltpu.SemaphoreType.DMA((30,)),
            pltpu.SemaphoreType.DMA,
            pltpu.SemaphoreType.REGULAR((2,)),
            pltpu.SemaphoreType.DMA,
            pltpu.SemaphoreType.DMA,
            pltpu.SemaphoreType.DMA,
            pltpu.SemaphoreType.DMA,
            pltpu.SemaphoreType.DMA,
            pltpu.SemaphoreType.DMA((3,)),
        ],
        compiler_params=pltpu.CompilerParams(collective_id=0, has_side_effects=True, vmem_limit_bytes=VMEM_LIMIT),
    )(
        *map(in_hbm, (
            slots,
            offset,
            group_var,
            deviation,
            deviation.reshape(2 * PERIODS, 128),
            footprint,
            observed.reshape(1, RECEPTORS),
            obs_group.reshape(1, RECEPTORS),
            inv_time,
            inv_lat,
            inv_lon,
        ))
    )
    total, second, misfit = pl.pallas_call(
        adjoint_kernel,
        name="adjoint",
        out_shape=(
            jax.ShapeDtypeStruct((SUM_ROWS, 8, 128), F32),
            jax.ShapeDtypeStruct((SUM_ROWS, 8, 128), F32),
            jax.ShapeDtypeStruct((1, RECEPTORS), F32),
        ),
        in_specs=[pl.BlockSpec(memory_space=pl.ANY)] * 3 + [vmem] * 4,
        input_output_aliases={5: 0, 6: 1},
        out_specs=(vmem, vmem, hbm),
        scratch_shapes=[
            pltpu.SMEM((2, 2, 128), jnp.int32),
            pltpu.SMEM((RECEPTORS,), jnp.int32),
            pltpu.SMEM((RECEPTORS,), F32),
            pltpu.SemaphoreType.DMA((4,)),
        ],
        compiler_params=pltpu.CompilerParams(vmem_limit_bytes=VMEM_LIMIT),
    )(slots_near, starts_near, misfit_row.reshape(RECEPTORS), packed, misfit_row, clear_one, clear_two)
    piece = (HALF, 8, 128)
    shape = (TILES // 2 + 1, 2, PERIODS, 8, 128)
    gradient = pl.pallas_call(
        scatter_kernel,
        name="scatter",
        out_shape=jax.ShapeDtypeStruct((PERIODS, 2, 128), F32),
        in_specs=[vmem] * 4,
        out_specs=vmem,
        scratch_shapes=[
            pltpu.VMEM((SIDE, 2, PERIODS, 8, 128), F32),
            pltpu.VMEM((4, SIDE, *piece), F32),
            pltpu.VMEM((4, SIDE, *piece), F32),
            pltpu.VMEM((4, 3, *piece), F32),
            pltpu.VMEM((3, *piece), F32),
            pltpu.VMEM((3, *piece), F32),
            pltpu.VMEM((4, 2, *piece), F32),
            pltpu.VMEM((4, 2, *piece), F32),
            pltpu.VMEM((4, 3, *piece), F32),
            pltpu.VMEM((3, *piece), F32),
            pltpu.VMEM((3, *piece), F32),
            pltpu.VMEM((PERIODS, 8, 128), F32),
            pltpu.SemaphoreType.DMA,
            pltpu.SemaphoreType.DMA((18,)),
        ],
        compiler_params=pltpu.CompilerParams(collective_id=1, has_side_effects=True, vmem_limit_bytes=VMEM_LIMIT),
    )(total.reshape(shape), second.reshape(shape), prior, lat)
    return gradient, misfit.reshape(RECEPTORS)


def solution(mesh):
    return jax.shard_map(
        shards,
        mesh=mesh,
        in_specs=(
            P(None, "rec", "tile"),
            P("rec", "tile", None, None, None, None),
            P("rec", "tile", None),
            P("rec"),
            P("rec"),
            P("rec"),
            P(),
            P(),
            P(),
            P("tile", None),
        ),
        out_specs=(P(None, "rec", "tile"), P("rec")),
        check_vma=False,
    )
```

```python
import functools

import jax
import jax.numpy as jnp
from jax import lax
from jax.experimental import pallas as pl
from jax.experimental.pallas import tpu as pltpu
from jax.sharding import PartitionSpec as P

MESH = pl.DeviceIdType.MESH
HIGHEST = lax.Precision.HIGHEST
F32 = jnp.float32
VMEM_LIMIT = 28 << 20

SIDE = 4
CORES = 2
PERIODS = 64
HALF = 32
WINDOW = 8
TILES = 8
ROWS = (TILES + 1) * PERIODS
SUM_ROWS = (TILES + 2) * PERIODS
RECEPTORS = 256
STRIPS = 8
GROUP = 16
UNROLL = 8
Z_NEAR = (2, 6, 1, 7)
Z_FAR = (4, 3, 5)
SENT_ROWS = 60 * 8 + 16
FAR_FIRST = (2, 1, 3)
NEAR_FIRST = (1, 3, 2)


def place():
    rec = lax.axis_index("rec")
    return rec // 8, (rec // 2) % SIDE, rec % 2, lax.axis_index("tile")


def rec_of(x, y, c):
    return ((x % SIDE) * SIDE + (y % SIDE)) * CORES + c


def tile_of(x, y):
    return 2 * (x % SIDE) + (y % SIDE) // 2


def pair_of(y, c):
    return pl.multiple_of(4 * ((y % SIDE) % 2) + 2 * c, 2)


def in_hbm(value):
    return pltpu.with_memory_space_constraint(value, pltpu.HBM)


def greet(peers):
    barrier = pltpu.get_barrier_semaphore()
    for peer in peers:
        pl.semaphore_signal(barrier, inc=1, device_id=peer, device_id_type=MESH)
    return barrier


def plane_peers(x, y, c, z):
    peers = [(rec_of(x, y, 1 - c), z)]
    peers += [(rec_of(x + d, y, c), z) for d in (1, 2, 3)]
    peers += [(rec_of(x, y + d, c), z) for d in (1, 2, 3)]
    return peers


def copy_to(src, dst, send, recv, peer):
    return pltpu.make_async_remote_copy(
        src_ref=src, dst_ref=dst, send_sem=send, recv_sem=recv, device_id=peer, device_id_type=MESH
    )


def forward_kernel(
    slots_hbm,
    starts_hbm,
    group_var_hbm,
    dev,
    dev_rows,
    foot,
    observed_hbm,
    group_hbm,
    inv_time_hbm,
    inv_lat_hbm,
    inv_lon_hbm,
    misfit_out,
    prior_out,
    lat_out,
    packed,
    clear_one,
    clear_two,
    slots_out,
    starts_out,
    slots,
    starts,
    group_var,
    observed,
    group,
    inv_time,
    inv_lat,
    inv_lon,
    i_sem,
    firsts,
    blocks,
    strip,
    sums,
    field,
    shares,
    own_share,
    send_sem,
    recv_sem,
    near_sem,
    token,
    z_send,
    z_recv,
    s_send,
    s_recv,
    f_sem,
    l_sem,
):
    x, y, c, z = place()
    me = rec_of(x, y, c)
    partner = (rec_of(x, y, 1 - c), z)
    peers = plane_peers(x, y, c, z) + [(me, (z + d) % STRIPS) for d in Z_NEAR]
    barrier = greet(peers)
    def spot(sx, sy, sc, first, count):
        return strip.at[
            pl.ds(pl.multiple_of(PERIODS * (1 + tile_of(sx, sy)) + first, HALF), count), pl.ds(pair_of(sy, sc), 2), :
        ]

    own_local = pltpu.make_async_copy(dev, spot(x, y, c, 0, PERIODS), l_sem.at[0])
    own_local.start()
    load_all = pltpu.make_async_copy(foot.at[:, 0], packed, f_sem)
    load_all.start()
    small = []
    for n, (src, dst) in enumerate((
        (inv_time_hbm, inv_time), (inv_lat_hbm, inv_lat), (slots_hbm, slots), (starts_hbm, starts),
        (group_var_hbm, group_var), (observed_hbm, observed), (group_hbm, group), (inv_lon_hbm, inv_lon),
        (slots_hbm, slots_out), (starts_hbm, starts_out),
    )):
        load = pltpu.make_async_copy(src, dst, i_sem.at[n])
        load.start()
        small.append(load)

    own_field = pltpu.make_async_copy(dev_rows, field.at[z], l_sem.at[1])
    own_field.start()
    own_local.wait()
    pl.semaphore_wait(barrier, len(peers))
    for n, d in enumerate((2, STRIPS - 2)):
        pl.semaphore_signal(token.at[n], inc=1, device_id=(me, (z + d) % STRIPS), device_id_type=MESH)

    count = [0]

    def send(src, where, peer):
        n = count[0]
        count[0] += 1
        copy_to(src, where, send_sem, recv_sem.at[n], peer).start()
        return n

    def share_with_partner(src, where):
        copy_to(src, where, send_sem, near_sem, partner).start()

    def arrived(n, where):
        copy_to(where, where, send_sem, recv_sem.at[n], partner).wait_recv()

    first_a, first_b = spot(x, y, c, 0, HALF), spot(x, y, c, HALF, HALF)
    first_both = spot(x, y, c, 0, PERIODS)
    in_a, in_b, far_a, far_b = {}, {}, {}, {}
    for d in FAR_FIRST:
        in_a[d] = send(first_a, spot(x, y, c, 0, HALF), (rec_of(x + d, y, c), z))
        in_b[d] = send(first_b, spot(x, y, c, HALF, HALF), (rec_of(x, y + d, c), z))
    for d in FAR_FIRST:
        far_a[0, d] = send(first_a, spot(x, y, c, 0, HALF), (rec_of(x, y + d, c), z))
        far_b[0, d] = send(first_b, spot(x, y, c, HALF, HALF), (rec_of(x + d, y, c), z))
    share_with_partner(first_both, first_both)

    def send_along(d):
        copy_to(dev_rows, field.at[z], z_send, z_recv, (me, (z + d) % STRIPS)).start()

    for d in Z_NEAR:
        send_along(d)

    strip[pl.ds(0, PERIODS)] = jnp.zeros((PERIODS, 8, 128), F32)
    for load in small:
        load.wait()

    wide = (lax.broadcasted_iota(jnp.int32, (2 * PERIODS, PERIODS), 0) // 2
            == lax.broadcasted_iota(jnp.int32, (2 * PERIODS, PERIODS), 1)).astype(F32)
    time_rows = jnp.dot(wide, inv_time[...], precision=HIGHEST, preferred_element_type=F32)
    time_both = lax.dot_general(time_rows, wide, (((1,), (1,)), ((), ())), precision=HIGHEST, preferred_element_type=F32)
    square = (2 * PERIODS, 2 * PERIODS)
    same = lax.broadcasted_iota(jnp.int32, square, 0) % 2 == lax.broadcasted_iota(jnp.int32, square, 1) % 2
    time_both = jnp.where(same, time_both, 0.0)
    for n in range(2):
        pick = (lax.broadcasted_iota(jnp.int32, (64, 128), 0) == 2 * me + n).astype(F32)
        lat_out[n] = jnp.dot(inv_lat[...], pick, precision=HIGHEST, preferred_element_type=F32)

    for m in range(2):
        pl.semaphore_wait(token.at[m], 1)
    for d in Z_FAR:
        send_along(d)

    for d in NEAR_FIRST:
        here = spot(x - d, y, c, 0, HALF)
        arrived(in_a[d], here)
        for e in FAR_FIRST:
            far_a[d, e] = send(here, here, (rec_of(x, y + e, c), z))
        share_with_partner(here, here)
        here = spot(x, y - d, c, HALF, HALF)
        arrived(in_b[d], here)
        for e in FAR_FIRST:
            far_b[d, e] = send(here, here, (rec_of(x + e, y, c), z))
        share_with_partner(here, here)

    def clear(i, carry):
        rows = pl.ds(pl.multiple_of(i * 16, 16), 16)
        clear_one[rows] = jnp.zeros((16, 8, 128), F32)
        clear_two[rows] = jnp.zeros((16, 8, 128), F32)
        return carry

    lax.fori_loop(0, SUM_ROWS // 16, clear, 0)
    load_all.wait()

    def widen(block, i, carry):
        r = block * 128 + i
        blocks[r] = packed[r].astype(F32)
        for k in range(2):
            firsts[2 * r + k] = (slots[block, k, i] + 1) * PERIODS + starts[r]
        return carry

    for block in range(2):
        lax.fori_loop(0, 128, functools.partial(widen, block), 0, unroll=4)
    for d in (0, *NEAR_FIRST):
        for e in NEAR_FIRST:
            here = spot(x - d, y - e, c, 0, HALF)
            arrived(far_a[d, e], here)
            share_with_partner(here, here)
            here = spot(x - e, y - d, c, HALF, HALF)
            arrived(far_b[d, e], here)
            share_with_partner(here, here)
    half_strip = strip.at[pl.ds(0, TILES * PERIODS // 2)]
    copy_to(half_strip, half_strip, send_sem, near_sem, partner).wait_recv()

    def group_sums(block, i, carry):
        totals = []
        for u in range(GROUP):
            r = block * 128 + i * GROUP + u
            parts = []
            for k in range(2):
                base = firsts[2 * r + k]
                parts.append(strip[pl.ds(base, WINDOW)] * blocks[r, k])
            totals.append(jnp.sum(parts[0] + parts[1], axis=0))
        sums[pl.ds(pl.multiple_of(block * 128 + i * GROUP, GROUP), GROUP), :] = jnp.sum(jnp.stack(totals), axis=1)
        return carry

    for block in range(2):
        lax.fori_loop(0, 128 // GROUP, functools.partial(group_sums, block), 0)
    share = lax.dot_general(
        jnp.ones((8, 128), F32), sums[...], (((1,), (1,)), ((), ())), precision=HIGHEST, preferred_element_type=F32
    )
    own_share[...] = share
    for d in Z_FAR + Z_NEAR:
        copy_to(
            own_share.at[pl.ds(0, 1), :], shares.at[pl.ds(z, 1), :], s_send, s_recv, (me, (z + d) % STRIPS)
        ).start()
    mine = pltpu.make_async_copy(own_share.at[pl.ds(0, 1), :], shares.at[pl.ds(z, 1), :], l_sem.at[2])
    mine.start()

    own_field.wait()
    others = field.at[pl.ds(0, STRIPS - 1)]
    copy_to(others, others, z_send, z_recv, partner).wait()
    lon_done = jnp.zeros((2 * PERIODS, 128), F32)
    for s in range(STRIPS):
        lon_done += lax.dot_general(
            field[s], inv_lon[:, s * 128 : (s + 1) * 128], (((1,), (1,)), ((), ())),
            precision=HIGHEST, preferred_element_type=F32,
        )
    prior_out[...] = jnp.dot(time_both, lon_done, precision=HIGHEST, preferred_element_type=F32)

    mine.wait()
    sent = strip.at[pl.ds(0, SENT_ROWS)]
    copy_to(sent, sent, send_sem, near_sem, partner).wait_send()
    others = shares.at[pl.ds(0, STRIPS - 1), :]
    copy_to(others, others, s_send, s_recv, partner).wait()
    predicted = jnp.sum(shares[...], axis=0, keepdims=True)
    variance = jnp.zeros((1, RECEPTORS), F32)
    for g in range(4):
        variance += jnp.where(group[...] == g, group_var[g], 0.0)
    misfit_out[...] = (predicted - observed[...]) / variance


def adjoint_kernel(
    slots_hbm, starts_hbm, misfit_hbm, blocks, misfit_row, clear_one, clear_two, total, second, misfit_out, slots, starts, misfit, i_sem
):
    small = []
    for n, (src, dst) in enumerate(((slots_hbm, slots), (starts_hbm, starts), (misfit_hbm, misfit))):
        load = pltpu.make_async_copy(src, dst, i_sem.at[n])
        load.start()
        small.append(load)
    result = pltpu.make_async_copy(misfit_row, misfit_out, i_sem.at[3])
    result.start()

    for load in small:
        load.wait()

    def pair(block, i, carry):
        held = []
        for u, into in ((0, total), (1, second)):
            r = block * 128 + 2 * i + u
            start = starts[r]
            weight = misfit[r]
            for k in range(2):
                rows = pl.ds((slots[block, k, 2 * i + u] + 2) * PERIODS + start, WINDOW)
                held.append((into, rows, into[rows] + blocks[r, k].astype(F32) * weight))
        for into, rows, value in held:
            into[rows] = value
        return carry

    for block in range(2):
        lax.fori_loop(0, 64, functools.partial(pair, block), 0, unroll=UNROLL)
    result.wait()


ORDER = (2, 1, 3, 0)


def scatter_kernel(
    total, second, prior, lat, out, part, a_swap, a_both, a_got, a_sum, a_last, b_swap, b_both, b_got, b_sum, b_last,
    done, send_sem, recv_sem,
):
    x, y, c, z = place()
    partner = (rec_of(x, y, 1 - c), z)
    peers = plane_peers(x, y, c, z)
    barrier = greet(peers)

    def one_period(p, carry):
        first = jnp.broadcast_to(prior[pl.ds(2 * p, 1), :], (8, 128))
        other = jnp.broadcast_to(prior[pl.ds(2 * p + 1, 1), :], (8, 128))
        for t in range(TILES):
            rows = slice(8 * t, 8 * t + 8)
            part[t // 2, t % 2, p] = (
                total[1 + t // 2, t % 2, p] + second[1 + t // 2, t % 2, p]
                + (lat[0, rows, :] * first + lat[1, rows, :] * other)
            )
        return carry

    lax.fori_loop(0, PERIODS, one_period, 0)
    pl.semaphore_wait(barrier, len(peers))

    first_half, second_half = pl.ds(0, HALF), pl.ds(HALF, HALF)
    def send(n, src, dst, peer):
        copy_to(src, dst, send_sem, recv_sem.at[n], peer).start()

    def arrived(n, where):
        copy_to(where, where, send_sem, recv_sem.at[n], partner).wait_recv()

    def pair_rows(sy, sc):
        return pl.ds(pair_of(sy, sc), 2)

    def half_of(sy):
        return (sy % SIDE) // 2

    mine = pair_rows(y, c)
    for e in ORDER:
        theirs = pair_rows(y + e, 1 - c)
        send(e, part.at[:, half_of(y + e), first_half, theirs, :], a_swap.at[e, :, :, theirs, :], partner)
        for h in range(2):
            rows = pl.ds(pl.multiple_of(4 * h + 2 * (1 - c), 2), 2)
            send(4 + e, part.at[(x + e) % SIDE, :, second_half, rows, :], b_swap.at[e, :, :, rows, :], partner)
    for e in ORDER:
        rows = pair_rows(y + e, c)
        arrived(e, a_swap.at[e, :, :, rows, :])
        for s in range(SIDE):
            a_both[e, s] = part[s, half_of(y + e), first_half] + a_swap[e, s]
        for d in FAR_FIRST:
            send(
                8 + e, a_both.at[e, (x + d) % SIDE, :, rows, :], a_got.at[e, d - 1, :, rows, :], (rec_of(x + d, y, c), z)
            )
        both_rows = b_swap.at[e, :, :, pl.ds(0, 4), :]
        arrived(4 + e, both_rows)
        for th in range(2):
            b_both[e, th] = part[(x + e) % SIDE, th, second_half] + b_swap[e, th]
        for d in FAR_FIRST:
            send(
                12 + e,
                b_both.at[e, half_of(y + d), :, pair_rows(y + d, c), :],
                b_got.at[e, d - 1, :, pair_rows(y + d, c), :],
                (rec_of(x, y + d, c), z),
            )
    for e in ORDER:
        rows = pair_rows(y + e, c)
        arrived(8 + e, a_got.at[e, :, :, rows, :])
        a_total = a_both[e, x] + a_got[e, 0] + a_got[e, 1] + a_got[e, 2]
        if e:
            a_sum[e - 1] = a_total
            send(16, a_sum.at[e - 1, :, rows, :], a_last.at[e - 1, :, rows, :], (rec_of(x, y + e, c), z))
        else:
            done[first_half] = a_total
        arrived(12 + e, b_got.at[e, :, :, mine, :])
        b_total = b_both[e, half_of(y)] + b_got[e, 0] + b_got[e, 1] + b_got[e, 2]
        if e:
            b_sum[e - 1] = b_total
            send(17, b_sum.at[e - 1, :, mine, :], b_last.at[e - 1, :, mine, :], (rec_of(x + e, y, c), z))
        else:
            done[second_half] = b_total
    sent = total.at[pl.ds(0, 4), :, pl.ds(0, 62), :, :]
    copy_to(sent, sent, send_sem, recv_sem.at[0], partner).wait_send()
    arrived(16, a_last.at[:, :, mine, :])
    out[first_half] = (
        done[first_half, mine, :] + a_last[0, :, mine, :] + a_last[1, :, mine, :] + a_last[2, :, mine, :]
    )
    arrived(17, b_last.at[:, :, mine, :])
    out[second_half] = (
        done[second_half, mine, :] + b_last[0, :, mine, :] + b_last[1, :, mine, :] + b_last[2, :, mine, :]
    )


def shards(
    deviation, footprint, tile_list, offset, observed, obs_group, group_var, inv_time, inv_lat, inv_lon
):
    vmem = pl.BlockSpec(memory_space=pltpu.VMEM)
    hbm = pl.BlockSpec(memory_space=pltpu.HBM)
    slots = jnp.transpose(tile_list.reshape(2, 128, 2), (0, 2, 1))
    misfit_row, prior, lat, packed, clear_one, clear_two, slots_near, starts_near = pl.pallas_call(
        forward_kernel,
        name="forward",
        out_shape=(
            jax.ShapeDtypeStruct((1, RECEPTORS), F32),
            jax.ShapeDtypeStruct((2 * PERIODS, 128), F32),
            jax.ShapeDtypeStruct((2, 64, 128), F32),
            jax.ShapeDtypeStruct((RECEPTORS, 2, WINDOW, 8, 128), jnp.bfloat16),
            jax.ShapeDtypeStruct((SUM_ROWS, 8, 128), F32),
            jax.ShapeDtypeStruct((SUM_ROWS, 8, 128), F32),
            jax.ShapeDtypeStruct((2, 2, 128), jnp.int32),
            jax.ShapeDtypeStruct((RECEPTORS,), jnp.int32),
        ),
        in_specs=[hbm] * 11,
        out_specs=(vmem,) * 8,
        scratch_shapes=[
            pltpu.SMEM((2, 2, 128), jnp.int32),
            pltpu.SMEM((RECEPTORS,), jnp.int32),
            pltpu.SMEM((4,), F32),
            pltpu.VMEM((1, RECEPTORS), F32),
            pltpu.VMEM((1, RECEPTORS), jnp.int32),
            pltpu.VMEM((PERIODS, PERIODS), F32),
            pltpu.VMEM((64, 64), F32),
            pltpu.VMEM((128, 1024), F32),
            pltpu.SemaphoreType.DMA((10,)),
            pltpu.SMEM((2 * RECEPTORS,), jnp.int32),
            pltpu.VMEM((RECEPTORS, 2, WINDOW, 8, 128), F32),
            pltpu.VMEM((ROWS, 8, 128), F32),
            pltpu.VMEM((RECEPTORS, 128), F32),
            pltpu.VMEM((STRIPS, 2 * PERIODS, 128), F32),
            pltpu.VMEM((STRIPS, RECEPTORS), F32),
            pltpu.VMEM((8, RECEPTORS), F32),
            pltpu.SemaphoreType.DMA,
            pltpu.SemaphoreType.DMA((30,)),
            pltpu.SemaphoreType.DMA,
            pltpu.SemaphoreType.REGULAR((2,)),
            pltpu.SemaphoreType.DMA,
            pltpu.SemaphoreType.DMA,
            pltpu.SemaphoreType.DMA,
            pltpu.SemaphoreType.DMA,
            pltpu.SemaphoreType.DMA,
            pltpu.SemaphoreType.DMA((3,)),
        ],
        compiler_params=pltpu.CompilerParams(collective_id=0, has_side_effects=True, vmem_limit_bytes=VMEM_LIMIT),
    )(
        *map(in_hbm, (
            slots,
            offset,
            group_var,
            deviation,
            deviation.reshape(2 * PERIODS, 128),
            footprint,
            observed.reshape(1, RECEPTORS),
            obs_group.reshape(1, RECEPTORS),
            inv_time,
            inv_lat,
            inv_lon,
        ))
    )
    total, second, misfit = pl.pallas_call(
        adjoint_kernel,
        name="adjoint",
        out_shape=(
            jax.ShapeDtypeStruct((SUM_ROWS, 8, 128), F32),
            jax.ShapeDtypeStruct((SUM_ROWS, 8, 128), F32),
            jax.ShapeDtypeStruct((1, RECEPTORS), F32),
        ),
        in_specs=[pl.BlockSpec(memory_space=pl.ANY)] * 3 + [vmem] * 4,
        input_output_aliases={5: 0, 6: 1},
        out_specs=(vmem, vmem, hbm),
        scratch_shapes=[
            pltpu.SMEM((2, 2, 128), jnp.int32),
            pltpu.SMEM((RECEPTORS,), jnp.int32),
            pltpu.SMEM((RECEPTORS,), F32),
            pltpu.SemaphoreType.DMA((4,)),
        ],
        compiler_params=pltpu.CompilerParams(vmem_limit_bytes=VMEM_LIMIT),
    )(slots_near, starts_near, misfit_row.reshape(RECEPTORS), packed, misfit_row, clear_one, clear_two)
    piece = (HALF, 8, 128)
    shape = (TILES // 2 + 1, 2, PERIODS, 8, 128)
    gradient = pl.pallas_call(
        scatter_kernel,
        name="scatter",
        out_shape=jax.ShapeDtypeStruct((PERIODS, 2, 128), F32),
        in_specs=[vmem] * 4,
        out_specs=vmem,
        scratch_shapes=[
            pltpu.VMEM((SIDE, 2, PERIODS, 8, 128), F32),
            pltpu.VMEM((4, SIDE, *piece), F32),
            pltpu.VMEM((4, SIDE, *piece), F32),
            pltpu.VMEM((4, 3, *piece), F32),
            pltpu.VMEM((3, *piece), F32),
            pltpu.VMEM((3, *piece), F32),
            pltpu.VMEM((4, 2, *piece), F32),
            pltpu.VMEM((4, 2, *piece), F32),
            pltpu.VMEM((4, 3, *piece), F32),
            pltpu.VMEM((3, *piece), F32),
            pltpu.VMEM((3, *piece), F32),
            pltpu.VMEM((PERIODS, 8, 128), F32),
            pltpu.SemaphoreType.DMA,
            pltpu.SemaphoreType.DMA((18,)),
        ],
        compiler_params=pltpu.CompilerParams(collective_id=1, has_side_effects=True, vmem_limit_bytes=VMEM_LIMIT),
    )(total.reshape(shape), second.reshape(shape), prior, lat)
    return gradient, misfit.reshape(RECEPTORS)


def solution(mesh):
    return jax.shard_map(
        shards,
        mesh=mesh,
        in_specs=(
            P(None, "rec", "tile"),
            P("rec", "tile", None, None, None, None),
            P("rec", "tile", None),
            P("rec"),
            P("rec"),
            P("rec"),
            P(),
            P(),
            P(),
            P("tile", None),
        ),
        out_specs=(P(None, "rec", "tile"), P("rec")),
        check_vma=False,
    )
```
